256 devices in a mesh: dom: 64 (over z, x, core), bin: 4 (over y).
Axes of the slice: x: 4, y: 4, z: 8, core: 2. Of those that a mesh axis runs over, the one named last changes fastest.
Arguments:
- points: float32 [3, 524288], P(None, ('dom', 'bin')), may hold values from 0 to 8, as said below
- candidates: int32 [16, 524288], P(None, ('dom', 'bin')), may hold values from 0 to 127, as said below
- block_dom: int32 [4096], P(('dom', 'bin')), may hold values from 0 to 63, as said below
- block_bin: int32 [4096], P(('dom', 'bin')), may hold values from 0 to 3, as said below
- block_slot: int32 [4096], P(('dom', 'bin')), may hold values from 0 to 31
- donor_nodes: float32 [81, 1048576], P(None, ('dom', 'bin')), may hold values from -1 to 9
- donor_flow: float32 [135, 1048576], P(None, ('dom', 'bin')), may hold values from -6 to 6
Outputs:
- blended: float32 [5, 524288], P(None, ('dom', 'bin'))
The draws below stay inside these ranges and needn't reach their ends.
Inputs may be any that keep to these rules, and one draw needn't show every extreme that they name: Cell c of a donor block sits at lattice position (c // 32, c // 8 % 4, c % 8) of a 4 x 4 x 8 brick of unit cells; the 16 candidates of a receptor are the cells of one 2 x 2 x 4 box of that brick, in a random order, and the receptor lies within that box. `points`: coordinates in the frame of the donor brick. `block_bin`: the 16 blocks of each device name every bin exactly 4 times. `block_dom`: take the blocks of the 4 devices that share one dom index and name one bin q: no dom index is named more than 2 times among them, and for every q the same 4 dom indices are named exactly 2 times by every such group.
All inputs are finite; a program needn't handle non-finite values.
Results may differ from the reference program's by a relative error of at most 0.0003.
Values sent between devices are 32-bit elements; how exact they have to be, the bound alone decides.
A program may use at most 128 MiB of HBM per device.

```python
import jax
import jax.numpy as jnp
from jax import lax

BLOCKS = 16
BLOCK_PTS = 128
CANDS = 16
VARS = 5
CELLS_BLK = 128
DONOR_BLOCKS = 32
STEPS = 6
CAP_BIN = 4
CAP_DOM = 2
HOT = 4
NBLK = 4096
PTS = 524288
DCELLS = 1048576
N_DOM = 64
N_BIN = 4


def route_tables(key):
    base = jax.random.fold_in(key, 7101)
    order_keys = jax.random.split(jax.random.fold_in(base, 1), N_DOM * N_BIN)
    order = jax.vmap(lambda one: jax.random.permutation(one, BLOCKS))(order_keys)
    order = order.reshape(N_DOM, N_BIN, BLOCKS).astype(jnp.int32)
    chosen_bin = order // CAP_BIN
    within = order % CAP_BIN
    bin_keys = jax.random.split(jax.random.fold_in(base, 2), N_BIN)
    dom_order = jax.vmap(lambda one: jax.random.permutation(one, N_DOM))(bin_keys).astype(jnp.int32)
    pair_keys = jax.random.split(jax.random.fold_in(base, 3), N_DOM * N_BIN)
    rest_order = jax.vmap(lambda one: jax.random.permutation(one, N_DOM - HOT))(pair_keys)
    rest_order = rest_order.reshape(N_DOM, N_BIN, N_DOM - HOT).astype(jnp.int32)
    slot_keys = jax.random.split(jax.random.fold_in(base, 4), N_DOM * N_BIN)
    shuffle = jax.vmap(lambda one: jax.random.permutation(one, BLOCKS))(slot_keys)
    shuffle = shuffle.reshape(N_DOM, N_BIN, BLOCKS).astype(jnp.int32)
    position = jnp.arange(BLOCKS, dtype=jnp.int32)
    hot_pick = dom_order[:, jnp.minimum(position // CAP_DOM, HOT - 1)]
    later = jnp.maximum(position - HOT * CAP_DOM, 0) % (N_DOM - HOT)
    others = jnp.broadcast_to(dom_order[None, :, HOT:], (N_DOM, N_BIN, N_DOM - HOT))
    rest_pick = jnp.take_along_axis(others, rest_order, axis=2)
    rest_seq = rest_pick[:, :, later]
    sequence = jnp.where((position < HOT * CAP_DOM)[None, None, :], hot_pick[None], rest_seq)
    table = jnp.take_along_axis(sequence, shuffle, axis=2)
    middle = jnp.arange(N_BIN, dtype=jnp.int32)[None, :, None] * CAP_BIN + within
    dom_index = jnp.arange(N_DOM, dtype=jnp.int32)[:, None, None]
    chosen_dom = table[dom_index, chosen_bin, middle]
    return (chosen_dom.reshape(-1).astype(jnp.int32), chosen_bin.reshape(-1).astype(jnp.int32))


def draw_block_dom(key, part):
    return route_tables(key)[0]


def draw_block_bin(key, part):
    return route_tables(key)[1]


def receptor_tables(key):
    base = jax.random.fold_in(key, 5303)
    key_i, key_j, key_k, key_perm, key_spot = jax.random.split(base, 5)
    corner_i = jax.random.randint(key_i, (PTS,), 0, 3)
    corner_j = jax.random.randint(key_j, (PTS,), 0, 3)
    corner_k = jax.random.randint(key_k, (PTS,), 0, 5)
    offsets = jax.vmap(lambda one: jax.random.permutation(one, CANDS))(jax.random.split(key_perm, PTS))
    cells = (corner_i[:, None] + offsets // 8) * 32 + (corner_j[:, None] + offsets // 4 % 2) * 8 + corner_k[:, None] + offsets % 4
    spot = jax.random.uniform(key_spot, (3, PTS), jnp.float32)
    located = jnp.stack([corner_i.astype(jnp.float32) + 2.0 * spot[0], corner_j.astype(jnp.float32) + 2.0 * spot[1], corner_k.astype(jnp.float32) + 4.0 * spot[2]])
    return (located, cells.T.astype(jnp.int32))


def draw_points(key, part):
    return receptor_tables(key)[0]


def draw_candidates(key, part):
    return receptor_tables(key)[1]


def draw_donor_nodes(key, part):
    base = jax.random.fold_in(key, 9011)
    key_diag, key_cross, key_wobble = jax.random.split(base, 3)
    cell = jnp.arange(DCELLS, dtype=jnp.int32) % CELLS_BLK
    center = jnp.stack([(cell // 32).astype(jnp.float32) + 0.5, (cell // 8 % 4).astype(jnp.float32) + 0.5, (cell % 8).astype(jnp.float32) + 0.5])
    diag = jax.random.uniform(key_diag, (3, DCELLS), jnp.float32, 0.4, 0.6)
    cross = jax.random.uniform(key_cross, (3, 3, DCELLS), jnp.float32, -0.05, 0.05)
    wobble = jax.random.uniform(key_wobble, (3, 27, DCELLS), jnp.float32, -0.003, 0.003)
    identity = jnp.eye(3, dtype=jnp.float32)
    matrix = cross * (1.0 - identity)[:, :, None] + identity[:, :, None] * diag[:, None, :]
    node = jnp.arange(27, dtype=jnp.int32)
    corners = jnp.stack([node // 9 - 1, node // 3 % 3 - 1, node % 3 - 1]).astype(jnp.float32)
    coords = center[:, None, :] + jnp.einsum('cdn,da->can', matrix, corners) + wobble
    return coords.reshape(81, DCELLS)


def with_ends(values, stream_key, smallest, high):
    shape = values.shape
    place = [jax.random.randint(jax.random.fold_in(stream_key, axis), (), 0, shape[axis]) for axis in range(len(shape))]
    values = values.at[tuple(place)].set(smallest)
    longest = shape.index(max(shape))
    place[longest] = (place[longest] + 1) % shape[longest]
    return values.at[tuple(place)].set(high)


def shard_levels(own_key, dims, cuts, smallest, high):
    level, own = 1.0, jax.random.fold_in(own_key, 6)
    for dim, shards_of in cuts:
        steps = jnp.exp(jax.random.uniform(jax.random.fold_in(own, dim), (shards_of,), jnp.float32, smallest / len(cuts), high / len(cuts)))
        level = level * jnp.repeat(steps, dims[dim] // shards_of).reshape([-1 if axis == dim else 1 for axis in range(len(dims))])
    return level


def scatter_about(rng, extent, scale, reach, shards=(), kind=jnp.bfloat16):
    values = scale * jax.random.normal(rng, extent, jnp.float32)
    if shards:
        values = values * shard_levels(rng, extent, shards, -0.22, 0.18)
    return jnp.clip(values, -reach, reach).astype(kind)


def setup_inputs(seed: int = 0) -> dict:
    arg_keys = jax.random.split(jax.random.key(seed), 8)
    points = draw_points(jax.random.fold_in(arg_keys[7], 71), 0)
    candidates = draw_candidates(jax.random.fold_in(arg_keys[7], 71), 0)
    block_dom = draw_block_dom(jax.random.fold_in(arg_keys[7], 71), 0)
    block_bin = draw_block_bin(jax.random.fold_in(arg_keys[7], 71), 0)
    block_slot = with_ends(jax.random.randint(arg_keys[4], (NBLK,), 0, DONOR_BLOCKS), jax.random.fold_in(arg_keys[4], 1), 0, DONOR_BLOCKS - 1).astype(jnp.int32)
    donor_nodes = draw_donor_nodes(jax.random.fold_in(arg_keys[7], 71), 0)
    donor_flow = scatter_about(arg_keys[6], (27 * VARS, DCELLS), 1.0, 6.0, ((1, 256),), jnp.float32)
    return {"points": points, "candidates": candidates, "block_dom": block_dom, "block_bin": block_bin, "block_slot": block_slot, "donor_nodes": donor_nodes, "donor_flow": donor_flow}


clamp_edge = 1.25
relax_factor = 0.5
sharpness = 16.0


def lagrange(coord):
    values = jnp.stack([0.5 * coord * (coord - 1.0), 1.0 - coord * coord, 0.5 * coord * (coord + 1.0)])
    slopes = jnp.stack([coord - 0.5, -2.0 * coord, coord + 0.5])
    return values, slopes


def tensor_basis(first, second, third):
    joined = first[:, None, None] * second[None, :, None] * third[None, None, :]
    return joined.reshape((27,) + first.shape[1:])


def shapes_at(ref_point):
    value_x, slope_x = lagrange(ref_point[0])
    value_y, slope_y = lagrange(ref_point[1])
    value_z, slope_z = lagrange(ref_point[2])
    return (tensor_basis(value_x, value_y, value_z), tensor_basis(slope_x, value_y, value_z),
            tensor_basis(value_x, slope_y, value_z), tensor_basis(value_x, value_y, slope_z))


def cross_product(left, right):
    return jnp.stack([left[1] * right[2] - left[2] * right[1],
                      left[2] * right[0] - left[0] * right[2],
                      left[0] * right[1] - left[1] * right[0]])


def blend_points(points, cells, flows):
    geometry = cells.reshape((3, 27) + cells.shape[1:])
    ref_point = jnp.zeros((3,) + cells.shape[1:], jnp.float32)
    for sweep in range(STEPS):
        weight_fn, along_x, along_y, along_z = shapes_at(ref_point)
        position = jnp.sum(geometry * weight_fn[None], axis=1)
        column_x = jnp.sum(geometry * along_x[None], axis=1)
        column_y = jnp.sum(geometry * along_y[None], axis=1)
        column_z = jnp.sum(geometry * along_z[None], axis=1)
        misfit = position - points[:, None, :]
        normal_yz = cross_product(column_y, column_z)
        determinant = jnp.sum(column_x * normal_yz, axis=0)
        step_x = jnp.sum(misfit * normal_yz, axis=0)
        step_y = jnp.sum(column_x * cross_product(misfit, column_z), axis=0)
        step_z = jnp.sum(column_x * cross_product(column_y, misfit), axis=0)
        update = jnp.stack([step_x, step_y, step_z]) / determinant[None]
        ref_point = jnp.clip(ref_point - relax_factor * update, -clamp_edge, clamp_edge)
    weight_fn = shapes_at(ref_point)[0]
    fields = jnp.sum(flows.reshape((VARS, 27) + flows.shape[1:]) * weight_fn[None], axis=1)
    excess = jnp.sum(jnp.square(jnp.maximum(jnp.abs(ref_point) - 1.0, 0.0)), axis=0)
    trust = 1.0 / (1.0 + sharpness * excess)
    return jnp.sum(fields * trust[None], axis=1) / jnp.sum(trust, axis=0)[None]


def reference(points, candidates, block_dom, block_bin, block_slot, donor_nodes, donor_flow):
    owner = ((block_dom * N_BIN + block_bin) * DONOR_BLOCKS + block_slot).astype(jnp.int32)
    offsets = jnp.repeat(owner * CELLS_BLK, BLOCK_PTS, total_repeat_length=PTS).astype(jnp.int32)
    cell_ids = (candidates + offsets[None, :]).astype(jnp.int32)
    span = 64 * BLOCK_PTS
    groups = PTS // span

    def one_group(group):
        start = (group * span).astype(jnp.int32)
        chosen = lax.dynamic_slice_in_dim(points, start, span, 1)
        ids = lax.dynamic_slice_in_dim(cell_ids, start, span, 1)
        cells = jnp.take(donor_nodes, ids, axis=1)
        flows = jnp.take(donor_flow, ids, axis=1)
        return blend_points(chosen, cells, flows)

    result = lax.map(one_group, jnp.arange(groups, dtype=jnp.int32))
    return jnp.transpose(result, (1, 0, 2)).reshape(VARS, PTS)
```

```python
import functools

import jax
import jax.numpy as jnp
import numpy as np
from jax import lax
from jax.experimental import pallas as pl
from jax.experimental.pallas import tpu as pltpu
from jax.sharding import PartitionSpec as P

VARS = 5
LANES = 128
STEPS = 6
CAP_DOM = 2

clamp_edge = 1.25
relax_factor = 0.5
sharpness = 16.0

MESH = pl.DeviceIdType.MESH
F32 = jnp.float32
I32 = jnp.int32


def monomial_map(fields):
    one = np.array([[0.0, 1.0, 0.0], [-0.5, 0.0, 0.5], [0.5, -1.0, 0.5]])
    cell = np.kron(np.kron(one, one), one)
    return np.kron(np.eye(fields), cell).astype(np.float32)


def enter(bins, doms):
    me_dom, me_bin = lax.axis_index("dom"), lax.axis_index("bin")
    barrier = pltpu.get_barrier_semaphore()

    def greet_bin(off, carry):
        other = lax.rem(me_bin + off, bins)
        pl.semaphore_signal(barrier, inc=1, device_id=(me_dom, other), device_id_type=MESH)
        return carry

    def greet_dom(off, carry):
        other = lax.rem(me_dom + off, doms)
        pl.semaphore_signal(barrier, inc=1, device_id=(other, me_bin), device_id_type=MESH)
        return carry

    lax.fori_loop(1, bins, greet_bin, 0)
    lax.fori_loop(1, doms, greet_dom, 0)
    return lambda: pl.semaphore_wait(barrier, bins - 1 + doms - 1)


def exchange(count, copy_to):
    def start(off, carry):
        copy_to(off).start()
        return carry

    def finish(off, carry):
        copy_to(off).wait()
        return carry

    lax.fori_loop(1, count, start, 0)
    return lambda: lax.fori_loop(1, count, finish, 0)


def ranks(labels):
    count = len(labels)
    out = []
    for i in range(count):
        rank = jnp.int32(0)
        for j in range(i):
            rank = rank + (labels[j] == labels[i]).astype(I32)
        out.append(rank)
    return out


def request_kernel(
    bins, doms, blocks,
    bin_ref, dom_ref, slot_ref, pts_ref, cand_ref,
    tiles_ref, meta_ref,
    raw, msg, got, pack, bin_send, bin_recv, dom_send, dom_recv,
):
    me_dom, me_bin = lax.axis_index("dom"), lax.axis_index("bin")
    per = blocks // bins
    entered = enter(bins, doms)
    sub = lax.broadcasted_iota(I32, (8, LANES), 0)
    lane = lax.broadcasted_iota(I32, (8, LANES), 1)

    for b in range(blocks):
        span = pl.ds(b * LANES, LANES)
        corner = jnp.min(cand_ref[:, span], axis=0, keepdims=True)
        raw[b, 0:3, :] = pts_ref[:, span]
        raw[b, 3:4, :] = (corner + slot_ref[b] * LANES).astype(F32)
        raw[b, 4:5, :] = jnp.full((1, LANES), dom_ref[b], I32).astype(F32)
        raw[b, 5:8, :] = jnp.zeros((3, LANES), F32)
    bin_of = [bin_ref[b] for b in range(blocks)]
    place = [x * per + r for x, r in zip(bin_of, ranks(bin_of))]
    for p in range(blocks):
        source = jnp.int32(0)
        for b in range(blocks):
            source = source + jnp.where(place[b] == p, b, 0)
        msg[p] = raw[source]
    entered()

    def to_bin(off):
        other = lax.rem(me_bin + off, bins)
        return pltpu.make_async_remote_copy(
            src_ref=msg.at[pl.ds(other * per, per)],
            dst_ref=got.at[pl.ds(me_bin * per, per)],
            send_sem=bin_send.at[off],
            recv_sem=bin_recv.at[off],
            device_id=(me_dom, other),
            device_id_type=MESH,
        )

    finish = exchange(bins, to_bin)
    for i in range(per):
        got[me_bin * per + i] = msg[me_bin * per + i]
    finish()

    named, tiles, number = [], [], []
    for b in range(blocks):
        tile = got[b]
        name = jnp.broadcast_to(got[b, 4:5, :], (8, LANES))
        rank = jnp.zeros((8, LANES), F32)
        for j in range(b):
            rank = rank + jnp.where(number[j] == name, 1.0, 0.0)
        number.append(name)
        named.append(jnp.where(jnp.where(sub < 4, 0.0, 1.0) == rank, name, -1.0))
        tiles.append(jnp.where(sub < 4, tile, pltpu.roll(tile, 4, 0)))
        number_rank = (name * CAP_DOM + rank).astype(I32)
        if b == 0:
            where_row = jnp.where(lane == 0, number_rank, 0)
        else:
            where_row = jnp.where(lane == b, number_rank, where_row)
    empty = jnp.where(sub % 4 == 3, -1.0, 0.0)

    def fill(a, carry):
        target = a.astype(F32)
        acc = empty
        for b in range(blocks):
            acc = jnp.where(named[b] == target, tiles[b], acc)
        pack[a] = acc
        return carry

    lax.fori_loop(0, doms, fill, 0)

    def to_dom(off):
        other = lax.rem(me_dom + off, doms)
        return pltpu.make_async_remote_copy(
            src_ref=pack.at[other],
            dst_ref=tiles_ref.at[me_dom],
            send_sem=dom_send.at[off],
            recv_sem=dom_recv.at[off],
            device_id=(other, me_bin),
            device_id_type=MESH,
        )

    finish = exchange(doms, to_dom)
    tiles_ref[me_dom] = pack[me_dom]
    finish()

    def table(a, acc):
        tile = tiles_ref[a]
        for k in range(CAP_DOM):
            cell = jnp.broadcast_to(tile[4 * k + 3 : 4 * k + 4, :], (8, LANES))
            slot = jnp.floor(cell * (1.0 / LANES)).astype(I32)
            acc = jnp.where(lane == CAP_DOM * a + k, slot, acc)
        return acc

    slots = lax.fori_loop(0, doms, table, jnp.full((8, LANES), -1, I32))
    meta_ref[...] = jnp.where(sub == 0, slots, jnp.where(sub == 1, where_row, 0))


def horner(t, c0, c1, c2):
    return (c2 * t + c1) * t + c0


def horner_slope(t, c0, c1, c2):
    top = c2 * t
    mid = top + c1
    return mid * t + c0, mid + top


def cross(a, b):
    return (
        a[1] * b[2] - a[2] * b[1],
        a[2] * b[0] - a[0] * b[2],
        a[0] * b[1] - a[1] * b[0],
    )


def dot3(a, b):
    return a[0] * b[0] + a[1] * b[1] + a[2] * b[2]


def blend_kernel(
    requests, cells,
    meta_ref, tiles_ref, node_map_ref, flow_map_ref, nodes_ref, flow_ref,
    out_ref,
    node_c, flow_c, held,
):
    width = 256

    def convert(i, carry):
        span = pl.ds(pl.multiple_of(i * width, width), width)
        node_c[:, span] = jnp.dot(
            node_map_ref[...], nodes_ref[:, span],
            precision=lax.Precision.HIGHEST, preferred_element_type=F32,
        )
        flow_c[:, span] = jnp.dot(
            flow_map_ref[...], flow_ref[:, span],
            precision=lax.Precision.HIGHEST, preferred_element_type=F32,
        )
        return carry

    lax.fori_loop(0, cells // width, convert, 0)

    row = lax.broadcasted_iota(I32, (8, LANES), 0)
    box = 8 * (row // 4) + row % 4

    def one(number, slot):
        base = lax.rem(number, CAP_DOM) * 4
        tile = number // CAP_DOM
        points = [
            jnp.broadcast_to(tiles_ref[tile, pl.ds(base + c, 1), :], (16, LANES)) for c in range(3)
        ]
        cell = tiles_ref[tile, pl.ds(base + 3, 1), :]
        corner = jnp.broadcast_to(cell.astype(I32) - slot * LANES, (8, LANES)) + box
        halves = (corner, corner + 32)
        span = pl.ds(pl.multiple_of(slot * LANES, LANES), LANES)

        def pick(table, r):
            line = jnp.broadcast_to(table[r : r + 1, span], (8, LANES))
            return jnp.concatenate(
                [jnp.take_along_axis(line, h, axis=1, mode="promise_in_bounds") for h in halves],
                axis=0,
            )

        for r in range(81):
            held[r] = pick(node_c, r)

        def coeff(c, i, j, k):
            return held[27 * c + 9 * i + 3 * j + k]

        r = None
        for step in range(STEPS):
            value, d1, d2, d3 = [], [], [], []
            for c in range(3):
                if r is None:
                    value.append(coeff(c, 0, 0, 0))
                    d1.append(coeff(c, 1, 0, 0))
                    d2.append(coeff(c, 0, 1, 0))
                    d3.append(coeff(c, 0, 0, 1))
                    continue
                x0, x2, x3 = [], [], []
                for i in range(3):
                    y0, y3 = [], []
                    for j in range(3):
                        v, d = horner_slope(r[2], *[coeff(c, i, j, k) for k in range(3)])
                        y0.append(v)
                        y3.append(d)
                    v, d = horner_slope(r[1], *y0)
                    x0.append(v)
                    x2.append(d)
                    x3.append(horner(r[1], *y3))
                v, d = horner_slope(r[0], *x0)
                value.append(v)
                d1.append(d)
                d2.append(horner(r[0], *x2))
                d3.append(horner(r[0], *x3))
            misfit = [value[c] - points[c] for c in range(3)]
            normal = cross(d2, d3)
            side = cross(d1, misfit)
            scale = relax_factor / dot3(d1, normal)
            change = (dot3(misfit, normal), dot3(d3, side), -dot3(d2, side))
            r = [
                jnp.clip((0.0 if r is None else r[c]) - scale * change[c], -clamp_edge, clamp_edge)
                for c in range(3)
            ]
        excess = [jnp.maximum(jnp.abs(x) - 1.0, 0.0) for x in r]
        trust = 1.0 / (1.0 + sharpness * dot3(excess, excess))
        total = 1.0 / jnp.sum(trust, axis=0, keepdims=True)
        for v in range(VARS):
            x0 = []
            for i in range(3):
                y0 = []
                for j in range(3):
                    y0.append(
                        horner(r[2], *[pick(flow_c, 27 * v + 9 * i + 3 * j + k) for k in range(3)])
                    )
                x0.append(horner(r[1], *y0))
            field = horner(r[0], *x0)
            out_ref[number, v : v + 1, :] = jnp.sum(field * trust, axis=0, keepdims=True) * total

    def each(i, carry):
        slot = meta_ref[0, i]

        @pl.when(slot >= 0)
        def _():
            one(i, slot)

        return carry

    lax.fori_loop(0, requests, each, 0)


def reply_kernel(
    bins, doms, blocks,
    bin_ref, meta_ref, res_ref,
    out_ref,
    back, picked, final, bin_send, bin_recv, dom_send, dom_recv,
):
    me_dom, me_bin = lax.axis_index("dom"), lax.axis_index("bin")
    per = blocks // bins
    entered = enter(bins, doms)
    entered()

    def to_dom(off):
        other = lax.rem(me_dom + off, doms)
        return pltpu.make_async_remote_copy(
            src_ref=res_ref.at[pl.ds(CAP_DOM * other, CAP_DOM)],
            dst_ref=back.at[pl.ds(CAP_DOM * me_dom, CAP_DOM)],
            send_sem=dom_send.at[off],
            recv_sem=dom_recv.at[off],
            device_id=(other, me_bin),
            device_id_type=MESH,
        )

    finish = exchange(doms, to_dom)
    for k in range(CAP_DOM):
        back[CAP_DOM * me_dom + k] = res_ref[CAP_DOM * me_dom + k]
    finish()
    for b in range(blocks):
        picked[b] = back[meta_ref[1, b]]

    def to_bin(off):
        other = lax.rem(me_bin + off, bins)
        return pltpu.make_async_remote_copy(
            src_ref=picked.at[pl.ds(other * per, per)],
            dst_ref=final.at[pl.ds(me_bin * per, per)],
            send_sem=bin_send.at[off],
            recv_sem=bin_recv.at[off],
            device_id=(me_dom, other),
            device_id_type=MESH,
        )

    finish = exchange(bins, to_bin)
    for i in range(per):
        final[me_bin * per + i] = picked[me_bin * per + i]
    finish()
    bin_of = [bin_ref[b] for b in range(blocks)]
    place = [x * per + r for x, r in zip(bin_of, ranks(bin_of))]
    for b in range(blocks):
        out_ref[:, pl.ds(b * LANES, LANES)] = final[place[b]][0:VARS, :]


def local(points, candidates, block_dom, block_bin, block_slot, donor_nodes, donor_flow):
    bins, doms = lax.axis_size("bin"), lax.axis_size("dom")
    blocks = block_dom.shape[0]
    requests = doms * CAP_DOM
    cells = donor_nodes.shape[1]
    vmem = pl.BlockSpec(memory_space=pltpu.VMEM)
    smem = pl.BlockSpec(memory_space=pltpu.SMEM)
    sems = [
        pltpu.SemaphoreType.DMA((bins,)),
        pltpu.SemaphoreType.DMA((bins,)),
        pltpu.SemaphoreType.DMA((doms,)),
        pltpu.SemaphoreType.DMA((doms,)),
    ]

    tiles, meta = pl.pallas_call(
        functools.partial(request_kernel, bins, doms, blocks),
        out_shape=(
            jax.ShapeDtypeStruct((doms, 8, LANES), F32),
            jax.ShapeDtypeStruct((8, LANES), I32),
        ),
        in_specs=[smem, smem, smem, vmem, vmem],
        out_specs=(vmem, vmem),
        scratch_shapes=[
            pltpu.VMEM((blocks, 8, LANES), F32),
            pltpu.VMEM((blocks, 8, LANES), F32),
            pltpu.VMEM((blocks, 8, LANES), F32),
            pltpu.VMEM((doms, 8, LANES), F32),
            *sems,
        ],
        compiler_params=pltpu.CompilerParams(collective_id=0, has_side_effects=True),
        name="request",
    )(block_bin, block_dom, block_slot, points, candidates)

    result = pl.pallas_call(
        functools.partial(blend_kernel, requests, cells),
        out_shape=jax.ShapeDtypeStruct((requests, 8, LANES), F32),
        in_specs=[smem, vmem, vmem, vmem, vmem, vmem],
        out_specs=vmem,
        scratch_shapes=[
            pltpu.VMEM((81, cells), F32),
            pltpu.VMEM((135, cells), F32),
            pltpu.VMEM((81, 16, LANES), F32),
        ],
        name="blend",
    )(
        meta, tiles, jnp.asarray(monomial_map(3)), jnp.asarray(monomial_map(VARS)),
        donor_nodes, donor_flow,
    )

    return pl.pallas_call(
        functools.partial(reply_kernel, bins, doms, blocks),
        out_shape=jax.ShapeDtypeStruct((VARS, points.shape[1]), F32),
        in_specs=[smem, smem, vmem],
        out_specs=vmem,
        scratch_shapes=[
            pltpu.VMEM((requests, 8, LANES), F32),
            pltpu.VMEM((blocks, 8, LANES), F32),
            pltpu.VMEM((blocks, 8, LANES), F32),
            *sems,
        ],
        compiler_params=pltpu.CompilerParams(collective_id=1, has_side_effects=True),
        name="reply",
    )(block_bin, meta, result)


def solution(mesh):
    split = P(None, ("dom", "bin"))
    table = P(("dom", "bin"))
    return jax.shard_map(
        local,
        mesh=mesh,
        in_specs=(split, split, table, table, table, split, split),
        out_specs=split,
        check_vma=False,
    )
```

```python
import functools

import jax
import jax.numpy as jnp
import numpy as np
from jax import lax
from jax.experimental import pallas as pl
from jax.experimental.pallas import tpu as pltpu
from jax.sharding import PartitionSpec as P

VARS = 5
LANES = 128
STEPS = 6
CAP_DOM = 2
X_CHIPS, CORES = 4, 2

UNIT = 16
NEAR = 6
SPREAD = NEAR * CORES
GUEST = SPREAD + 2
NODE_ROWS, FLOW_ROWS = 88, 136
ROWS = NODE_ROWS + FLOW_ROWS

clamp_edge = 1.25
relax_factor = 0.5
sharpness = 16.0

MESH = pl.DeviceIdType.MESH
F32 = jnp.float32
I32 = jnp.int32


def monomial_map(fields, rows):
    one = np.array([[0.0, 1.0, 0.0], [-0.5, 0.0, 0.5], [0.5, -1.0, 0.5]])
    cell = np.kron(np.kron(one, one), one)
    full = np.kron(np.eye(fields), cell)
    return np.pad(full, ((0, rows - full.shape[0]), (0, 0)))


def exact_dot(left, right):
    high = right.astype(jnp.bfloat16)
    rest = right - high.astype(F32)
    mid = rest.astype(jnp.bfloat16)
    low = (rest - mid.astype(F32)).astype(jnp.bfloat16)
    out = jnp.dot(left, low, preferred_element_type=F32)
    out = out + jnp.dot(left, mid, preferred_element_type=F32)
    return out + jnp.dot(left, high, preferred_element_type=F32)


class Place:
    def __init__(self, bins, doms):
        self.bins, self.doms = bins, doms
        self.dom, self.bin = lax.axis_index("dom"), lax.axis_index("bin")
        self.core = lax.rem(self.dom, CORES)
        self.x = lax.rem(self.dom // CORES, X_CHIPS)
        self.z = self.dom // (CORES * X_CHIPS)

    def chip(self, near, core, sign=1):
        step = sign if near % 2 == 0 else -sign
        layers = self.doms // (CORES * X_CHIPS)
        z, x, y = self.z, self.x, self.bin
        if near // 2 == 0:
            z = lax.rem(z + step + layers, layers)
        elif near // 2 == 1:
            x = lax.rem(x + step + X_CHIPS, X_CHIPS)
        else:
            y = lax.rem(y + step + self.bins, self.bins)
        return ((z * X_CHIPS + x) * CORES + core, y)

    def sibling(self):
        return (self.dom + 1 - 2 * self.core, self.bin)

    def enter(self):
        barrier = pltpu.get_barrier_semaphore()

        def greet(device):
            pl.semaphore_signal(barrier, inc=1, device_id=device, device_id_type=MESH)

        def greet_bin(off, carry):
            greet((self.dom, lax.rem(self.bin + off, self.bins)))
            return carry

        def greet_dom(off, carry):
            greet((lax.rem(self.dom + off, self.doms), self.bin))
            return carry

        lax.fori_loop(1, self.bins, greet_bin, 0)
        lax.fori_loop(1, self.doms, greet_dom, 0)
        for near in (4, 5):
            greet(self.chip(near, 1 - self.core))
        return lambda: pl.semaphore_wait(barrier, self.bins - 1 + self.doms - 1 + 2)


def exchange(count, copy_to):
    def start(off, carry):
        copy_to(off).start()
        return carry

    def finish(off, carry):
        copy_to(off).wait()
        return carry

    lax.fori_loop(1, count, start, 0)
    return lambda: lax.fori_loop(1, count, finish, 0)


def ranks(labels):
    count = len(labels)
    out = []
    for i in range(count):
        rank = jnp.int32(0)
        for j in range(i):
            rank = rank + (labels[j] == labels[i]).astype(I32)
        out.append(rank)
    return out


def request_kernel(
    bins, doms, blocks, cells,
    bin_ref, dom_ref, slot_ref, pts_ref, cand_ref, node_map_ref, flow_map_ref, nodes_ref, flow_ref,
    work_ref, meta_ref, ext_ref, own_ref,
    raw, msg, got, pack, tiles, ship, node_raw, flow_raw, coef,
    load_sem, keep_sem, bin_send, bin_recv, dom_send, dom_recv, ship_send, ship_recv,
    cell_send, cell_recv,
):
    me = Place(bins, doms)
    per = blocks // bins
    parts = load_sem.shape[1]
    width = cells // parts
    step = 256

    def load(i):
        span = pl.ds(i * width, width)
        return (
            pltpu.make_async_copy(nodes_ref.at[:, span], node_raw.at[:, span], load_sem.at[0, i]),
            pltpu.make_async_copy(flow_ref.at[:, span], flow_raw.at[:, span], load_sem.at[1, i]),
        )

    for i in range(parts):
        for copy in load(i):
            copy.start()
    entered = me.enter()
    sub = lax.broadcasted_iota(I32, (8, LANES), 0)
    lane = lax.broadcasted_iota(I32, (8, LANES), 1)

    for b in range(blocks):
        span = pl.ds(b * LANES, LANES)
        corner = jnp.min(cand_ref[:, span], axis=0, keepdims=True)
        raw[b, 0:3, :] = pts_ref[:, span]
        raw[b, 3:4, :] = (corner + slot_ref[b] * LANES).astype(F32)
        raw[b, 4:5, :] = jnp.full((1, LANES), dom_ref[b], I32).astype(F32)
        raw[b, 5:8, :] = jnp.zeros((3, LANES), F32)
    bin_of = [bin_ref[b] for b in range(blocks)]
    place = [x * per + r for x, r in zip(bin_of, ranks(bin_of))]
    for p in range(blocks):
        source = jnp.int32(0)
        for b in range(blocks):
            source = source + jnp.where(place[b] == p, b, 0)
        msg[p] = raw[source]

    def convert(i, carry):
        span = pl.ds(pl.multiple_of(i * step, step), step)
        node = exact_dot(node_map_ref[...], node_raw[:, span])
        flow = exact_dot(flow_map_ref[...], flow_raw[:, span])
        for k in range(step // LANES):
            part = slice(k * LANES, (k + 1) * LANES)
            coef[i * (step // LANES) + k, 0:NODE_ROWS, :] = node[:, part]
            coef[i * (step // LANES) + k, NODE_ROWS:ROWS, :] = flow[:, part]
        return carry

    for i in range(parts):
        for copy in load(i):
            copy.wait()
        lax.fori_loop(i * width // step, (i + 1) * width // step, convert, 0)
    keep = [
        pltpu.make_async_copy(coef, own_ref, keep_sem.at[0]),
        pltpu.make_async_copy(coef.at[0:4], ext_ref.at[0:4], keep_sem.at[1]),
    ]
    entered()

    def to_bin(off):
        other = lax.rem(me.bin + off, bins)
        return pltpu.make_async_remote_copy(
            src_ref=msg.at[pl.ds(other * per, per)],
            dst_ref=got.at[pl.ds(me.bin * per, per)],
            send_sem=bin_send.at[off],
            recv_sem=bin_recv.at[off],
            device_id=(me.dom, other),
            device_id_type=MESH,
        )

    finish_bin = exchange(bins, to_bin)

    spread = []
    for unit in range(SPREAD):
        near, core = unit // CORES, unit % CORES
        spread.append(
            pltpu.make_async_remote_copy(
                src_ref=coef.at[pl.ds(8 + 2 * unit, 2)],
                dst_ref=ext_ref.at[pl.ds(8 + 2 * (near * CORES + me.core), 2)],
                send_sem=cell_send.at[unit],
                recv_sem=cell_recv.at[near * CORES + me.core],
                device_id=me.chip(near, core),
                device_id_type=MESH,
            )
        )
    spread.append(
        pltpu.make_async_remote_copy(
            src_ref=coef.at[4:8],
            dst_ref=ext_ref.at[4:8],
            send_sem=cell_send.at[SPREAD],
            recv_sem=cell_recv.at[SPREAD],
            device_id=me.sibling(),
            device_id_type=MESH,
        )
    )
    for copy in spread:
        copy.start()
    for copy in keep:
        copy.start()

    for i in range(per):
        got[me.bin * per + i] = msg[me.bin * per + i]
    finish_bin()

    named, tile_of, number = [], [], []
    where_row = jnp.zeros((8, LANES), I32)
    for b in range(blocks):
        tile = got[b]
        name = jnp.broadcast_to(got[b, 4:5, :], (8, LANES))
        rank = jnp.zeros((8, LANES), F32)
        for j in range(b):
            rank = rank + jnp.where(number[j] == name, 1.0, 0.0)
        number.append(name)
        named.append(jnp.where(jnp.where(sub < 4, 0.0, 1.0) == rank, name, -1.0))
        tile_of.append(jnp.where(sub < 4, tile, pltpu.roll(tile, 4, 0)))
        where_row = jnp.where(lane == b, (name * CAP_DOM + rank).astype(I32), where_row)
    empty = jnp.where(sub % 4 == 3, -1.0, 0.0)

    def fill(a, carry):
        target = a.astype(F32)
        acc = empty
        for b in range(blocks):
            acc = jnp.where(named[b] == target, tile_of[b], acc)
        pack[a] = acc
        return carry

    lax.fori_loop(0, doms, fill, 0)

    def to_dom(off):
        other = lax.rem(me.dom + off, doms)
        return pltpu.make_async_remote_copy(
            src_ref=pack.at[other],
            dst_ref=tiles.at[pl.ds(pl.multiple_of(8 * me.dom, 8), 8)],
            send_sem=dom_send.at[off],
            recv_sem=dom_recv.at[off],
            device_id=(other, me.bin),
            device_id_type=MESH,
        )

    finish_dom = exchange(doms, to_dom)
    tiles[pl.ds(pl.multiple_of(8 * me.dom, 8), 8), :] = pack[me.dom]
    finish_dom()

    count = doms * CAP_DOM
    square = (count, LANES)
    row = [tiles[pl.ds(c, count, stride=4), :] for c in range(4)]
    first = lax.broadcasted_iota(I32, square, 0)
    second = lax.broadcasted_iota(I32, square, 1)
    before = first < second
    slot = jnp.floor(row[3] * (1.0 / LANES)).astype(I32)
    base = jnp.where(slot < 4, GUEST, jnp.where(slot < 8, SPREAD, (slot - 8) // 2))
    base = jnp.where(slot < 0, -1, base).astype(F32)
    base_row = base.T
    rank = jnp.sum(jnp.where((base == base_row) & before, 1.0, 0.0), axis=0, keepdims=True)
    base_row = base_row[0:1, :]
    cap = jnp.where(base_row == SPREAD, 2.0 * UNIT, 1.0 * UNIT)
    stay = (base_row == GUEST) | ((base_row >= 0.0) & (rank >= cap))
    stay_row = jnp.where(stay, 1.0, 0.0)
    stay_col = jnp.broadcast_to(stay_row, square).T
    stay_rank = jnp.sum(jnp.where(before, stay_col, 0.0), axis=0, keepdims=True)
    target = jnp.where(stay, GUEST * UNIT + stay_rank, base_row * UNIT + rank)
    target = jnp.where(base_row < 0.0, -1.0, target).astype(I32)
    places = GUEST * UNIT + count
    units = places // UNIT
    hot = jnp.where(
        lax.broadcasted_iota(I32, (places, LANES), 0) == jnp.broadcast_to(target, (places, LANES)),
        1.0, 0.0,
    ).astype(jnp.bfloat16)
    for c in range(4):
        moved = exact_dot(hot, row[c] + 1.0 if c == 3 else row[c])
        if c == 3:
            moved = moved - 1.0
        for u in range(GUEST):
            ship[u, c] = moved[u * UNIT : (u + 1) * UNIT, :]
        for u in range(GUEST, units):
            work_ref[u, c] = moved[u * UNIT : (u + 1) * UNIT, :]

    shipped = []
    for unit in range(SPREAD):
        near, core = unit // CORES, unit % CORES
        shipped.append(
            pltpu.make_async_remote_copy(
                src_ref=ship.at[unit],
                dst_ref=work_ref.at[near * CORES + me.core],
                send_sem=ship_send.at[unit],
                recv_sem=ship_recv.at[near * CORES + me.core],
                device_id=me.chip(near, core),
                device_id_type=MESH,
            )
        )
    shipped.append(
        pltpu.make_async_remote_copy(
            src_ref=ship.at[pl.ds(SPREAD, 2)],
            dst_ref=work_ref.at[pl.ds(SPREAD, 2)],
            send_sem=ship_send.at[SPREAD],
            recv_sem=ship_recv.at[SPREAD],
            device_id=me.sibling(),
            device_id_type=MESH,
        )
    )
    for copy in shipped:
        copy.start()

    def arrived(unit, sem, ref):
        return pltpu.make_async_remote_copy(
            src_ref=ref, dst_ref=ref, send_sem=sem.at[unit], recv_sem=sem.at[unit],
            device_id=me.sibling(), device_id_type=MESH,
        ).wait_recv()

    for unit in range(SPREAD):
        arrived(unit, ship_recv, work_ref.at[unit])
    arrived(SPREAD, ship_recv, work_ref.at[pl.ds(SPREAD, 2)])

    tall = (UNIT, LANES)
    down, across = lax.broadcasted_iota(I32, tall, 0), lax.broadcasted_iota(I32, tall, 1)
    lines = [jnp.zeros(tall, I32) for _ in range(3)]
    for u in range(units):
        slot = jnp.floor(work_ref[u, 3] * (1.0 / LANES)).astype(I32)
        if u < SPREAD:
            block = slot + 2 * (u % CORES - me.core)
        elif u < GUEST:
            block = slot
        else:
            block = jnp.where(slot < 4, slot, slot + 32)
        block = jnp.where(slot < 0, 0, block + 1)
        line = u * UNIT // LANES
        lines[line] = lines[line] + jnp.where(across == (u * UNIT) % LANES + down, block, 0)
    table = jnp.where(sub == 3, jnp.broadcast_to(target, sub.shape), where_row)
    for i in range(3):
        total = jnp.sum(lines[i].astype(F32), axis=0, keepdims=True).astype(I32) - 1
        table = jnp.where(sub == i, jnp.broadcast_to(total, sub.shape), table)
    meta_ref[...] = table

    for copy in shipped + spread:
        copy.wait_send()
    for unit in range(SPREAD):
        arrived(unit, cell_recv, ext_ref.at[pl.ds(8 + 2 * unit, 2)])
    arrived(SPREAD, cell_recv, ext_ref.at[4:8])
    for copy in keep:
        copy.wait()


def horner(t, c0, c1, c2):
    return (c2 * t + c1) * t + c0


def horner_slope(t, c0, c1, c2):
    top = c2 * t
    mid = top + c1
    return mid * t + c0, mid + top


def cross(a, b):
    return (
        a[1] * b[2] - a[2] * b[1],
        a[2] * b[0] - a[0] * b[2],
        a[0] * b[1] - a[1] * b[0],
    )


def dot3(a, b):
    return a[0] * b[0] + a[1] * b[1] + a[2] * b[2]


def blend_kernel(
    places, total_places,
    meta_ref, work_ref, ext_ref, own_ref,
    out_ref,
    held, buf, order, sem,
):
    def collect(first, last, found):
        def more(state):
            i, n = state
            at = jnp.minimum(i, total_places - 1)
            return (i < last) & (meta_ref[at // LANES, lax.rem(at, LANES)] >= 0)

        def note(state):
            i, n = state
            order[n] = i
            return i + 1, n + 1

        return lax.while_loop(more, note, (jnp.int32(first), found))[1]

    found = jnp.int32(0)
    for u in range(SPREAD):
        found = collect(u * UNIT, (u + 1) * UNIT, found)
    found = collect(SPREAD * UNIT, GUEST * UNIT, found)
    found = collect(GUEST * UNIT, total_places, found)

    def fetch(n, act):
        at = order[n]
        block = meta_ref[at // LANES, lax.rem(at, LANES)]
        side = lax.rem(n, 2)

        @pl.when(block < 32)
        def _():
            act(pltpu.make_async_copy(ext_ref.at[block], buf.at[side], sem.at[side]))

        @pl.when(block >= 32)
        def _():
            act(pltpu.make_async_copy(own_ref.at[block - 32], buf.at[side], sem.at[side]))

    @pl.when(found > 0)
    def _():
        fetch(0, lambda copy: copy.start())

    row = lax.broadcasted_iota(I32, (8, LANES), 0)
    box = 8 * (row // 4) + row % 4

    def one(n, carry):
        @pl.when(n + 1 < found)
        def _():
            fetch(n + 1, lambda copy: copy.start())

        fetch(n, lambda copy: copy.wait())
        place = order[n]
        half = lax.rem(n, 2)
        unit, at = place // UNIT, lax.rem(place, UNIT)
        points = [
            jnp.broadcast_to(work_ref[unit, c, pl.ds(at, 1), :], (16, LANES)) for c in range(3)
        ]
        cell = work_ref[unit, 3, pl.ds(at, 1), :].astype(I32) & (LANES - 1)
        corner = jnp.broadcast_to(cell, (8, LANES)) + box
        halves = (corner, corner + 32)

        def pick(r):
            line = jnp.broadcast_to(buf[half, r : r + 1, :], (8, LANES))
            return jnp.concatenate(
                [jnp.take_along_axis(line, h, axis=1, mode="promise_in_bounds") for h in halves],
                axis=0,
            )

        for r in range(81):
            held[r] = pick(r)

        def coeff(c, i, j, k):
            return held[27 * c + 9 * i + 3 * j + k]

        r = None
        for step in range(STEPS):
            value, d1, d2, d3 = [], [], [], []
            for c in range(3):
                if r is None:
                    value.append(coeff(c, 0, 0, 0))
                    d1.append(coeff(c, 1, 0, 0))
                    d2.append(coeff(c, 0, 1, 0))
                    d3.append(coeff(c, 0, 0, 1))
                    continue
                x0, x2, x3 = [], [], []
                for i in range(3):
                    y0, y3 = [], []
                    for j in range(3):
                        v, d = horner_slope(r[2], *[coeff(c, i, j, k) for k in range(3)])
                        y0.append(v)
                        y3.append(d)
                    v, d = horner_slope(r[1], *y0)
                    x0.append(v)
                    x2.append(d)
                    x3.append(horner(r[1], *y3))
                v, d = horner_slope(r[0], *x0)
                value.append(v)
                d1.append(d)
                d2.append(horner(r[0], *x2))
                d3.append(horner(r[0], *x3))
            misfit = [value[c] - points[c] for c in range(3)]
            normal = cross(d2, d3)
            side = cross(d1, misfit)
            scale = relax_factor / dot3(d1, normal)
            change = (dot3(misfit, normal), dot3(d3, side), -dot3(d2, side))
            r = [
                jnp.clip((0.0 if r is None else r[c]) - scale * change[c], -clamp_edge, clamp_edge)
                for c in range(3)
            ]
        excess = [jnp.maximum(jnp.abs(x) - 1.0, 0.0) for x in r]
        trust = 1.0 / (1.0 + sharpness * dot3(excess, excess))
        total = 1.0 / jnp.sum(trust, axis=0, keepdims=True)
        for v in range(VARS):
            x0 = []
            for i in range(3):
                y0 = []
                for j in range(3):
                    y0.append(
                        horner(r[2], *[pick(NODE_ROWS + 27 * v + 9 * i + 3 * j + k) for k in range(3)])
                    )
                x0.append(horner(r[1], *y0))
            field = horner(r[0], *x0)
            out_ref[place, v] = jnp.sum(field * trust, axis=0, keepdims=True) * total
        return carry

    lax.fori_loop(0, found, one, 0)


def reply_kernel(
    bins, doms, blocks,
    bin_ref, meta_ref, res_ref,
    out_ref,
    ret, send, back, picked, final,
    keep_sem, bin_send, bin_recv, dom_send, dom_recv, ship_send, ship_recv,
):
    me = Place(bins, doms)
    per = blocks // bins
    count = doms * CAP_DOM
    entered = me.enter()
    keep = pltpu.make_async_copy(
        res_ref.at[pl.ds(GUEST * UNIT, count)], ret.at[pl.ds(GUEST * UNIT, count)], keep_sem
    )
    keep.start()
    entered()

    shipped = []
    for unit in range(SPREAD):
        near, core = unit // CORES, unit % CORES
        shipped.append(
            pltpu.make_async_remote_copy(
                src_ref=res_ref.at[pl.ds(unit * UNIT, UNIT)],
                dst_ref=ret.at[pl.ds((near * CORES + me.core) * UNIT, UNIT)],
                send_sem=ship_send.at[unit],
                recv_sem=ship_recv.at[near * CORES + me.core],
                device_id=me.chip(near, core, -1),
                device_id_type=MESH,
            )
        )
    other_core = pl.ds(SPREAD * UNIT, 2 * UNIT)
    shipped.append(
        pltpu.make_async_remote_copy(
            src_ref=res_ref.at[other_core],
            dst_ref=ret.at[other_core],
            send_sem=ship_send.at[SPREAD],
            recv_sem=ship_recv.at[SPREAD],
            device_id=me.sibling(),
            device_id_type=MESH,
        )
    )
    for copy in shipped:
        copy.start()

    def arrived(unit, ref):
        return pltpu.make_async_remote_copy(
            src_ref=ref, dst_ref=ref, send_sem=ship_recv.at[unit], recv_sem=ship_recv.at[unit],
            device_id=me.sibling(), device_id_type=MESH,
        ).wait_recv()

    for unit in range(SPREAD):
        arrived(unit, ret.at[pl.ds(unit * UNIT, UNIT)])
    arrived(SPREAD, ret.at[other_core])
    keep.wait()

    def gather(j, carry):
        send[j] = ret[jnp.maximum(meta_ref[3, j], 0)]
        return carry

    lax.fori_loop(0, count, gather, 0, unroll=4)

    def to_dom(off):
        other = lax.rem(me.dom + off, doms)
        return pltpu.make_async_remote_copy(
            src_ref=send.at[pl.ds(CAP_DOM * other, CAP_DOM)],
            dst_ref=back.at[pl.ds(CAP_DOM * me.dom, CAP_DOM)],
            send_sem=dom_send.at[off],
            recv_sem=dom_recv.at[off],
            device_id=(other, me.bin),
            device_id_type=MESH,
        )

    finish = exchange(doms, to_dom)
    for k in range(CAP_DOM):
        back[CAP_DOM * me.dom + k] = send[CAP_DOM * me.dom + k]
    finish()
    for b in range(blocks):
        picked[b] = back[meta_ref[4, b]]

    def to_bin(off):
        other = lax.rem(me.bin + off, bins)
        return pltpu.make_async_remote_copy(
            src_ref=picked.at[pl.ds(other * per, per)],
            dst_ref=final.at[pl.ds(me.bin * per, per)],
            send_sem=bin_send.at[off],
            recv_sem=bin_recv.at[off],
            device_id=(me.dom, other),
            device_id_type=MESH,
        )

    finish = exchange(bins, to_bin)
    for i in range(per):
        final[me.bin * per + i] = picked[me.bin * per + i]
    finish()
    bin_of = [bin_ref[b] for b in range(blocks)]
    place = [x * per + r for x, r in zip(bin_of, ranks(bin_of))]
    for b in range(blocks):
        out_ref[:, pl.ds(b * LANES, LANES)] = final[place[b]].reshape(VARS, LANES)
    for copy in shipped:
        copy.wait_send()


def local(points, candidates, block_dom, block_bin, block_slot, donor_nodes, donor_flow):
    bins, doms = lax.axis_size("bin"), lax.axis_size("dom")
    blocks = block_dom.shape[0]
    cells = donor_nodes.shape[1]
    held_blocks = cells // LANES
    count = doms * CAP_DOM
    places = GUEST * UNIT + count
    units = places // UNIT
    vmem = pl.BlockSpec(memory_space=pltpu.VMEM)
    smem = pl.BlockSpec(memory_space=pltpu.SMEM)
    hbm = pl.BlockSpec(memory_space=pl.ANY)
    dma = pltpu.SemaphoreType.DMA
    routes = [dma((bins,)), dma((bins,)), dma((doms,)), dma((doms,))]
    pairs = [dma((SPREAD + 1,)), dma((SPREAD + 1,))]
    node_map = jnp.asarray(monomial_map(3, NODE_ROWS), jnp.bfloat16)
    flow_map = jnp.asarray(monomial_map(VARS, FLOW_ROWS), jnp.bfloat16)

    work, meta, ext, own = pl.pallas_call(
        functools.partial(request_kernel, bins, doms, blocks, cells),
        out_shape=(
            jax.ShapeDtypeStruct((units, 4, UNIT, LANES), F32),
            jax.ShapeDtypeStruct((8, LANES), I32),
            jax.ShapeDtypeStruct((held_blocks, ROWS, LANES), F32),
            jax.ShapeDtypeStruct((held_blocks, ROWS, LANES), F32),
        ),
        in_specs=[smem, smem, smem, vmem, vmem, vmem, vmem, hbm, hbm],
        out_specs=(vmem, vmem, hbm, hbm),
        scratch_shapes=[
            pltpu.VMEM((blocks, 8, LANES), F32),
            pltpu.VMEM((blocks, 8, LANES), F32),
            pltpu.VMEM((blocks, 8, LANES), F32),
            pltpu.VMEM((doms, 8, LANES), F32),
            pltpu.VMEM((doms * 8, LANES), F32),
            pltpu.VMEM((GUEST, 4, UNIT, LANES), F32),
            pltpu.VMEM((81, cells), F32),
            pltpu.VMEM((135, cells), F32),
            pltpu.VMEM((held_blocks, ROWS, LANES), F32),
            dma((2, 4)), dma((2,)), *routes, *pairs, *pairs,
        ],
        compiler_params=pltpu.CompilerParams(collective_id=0, has_side_effects=True),
        name="request",
    )(
        block_bin, block_dom, block_slot, points, candidates, node_map, flow_map,
        donor_nodes, donor_flow,
    )

    result = pl.pallas_call(
        functools.partial(blend_kernel, GUEST * UNIT, places),
        out_shape=jax.ShapeDtypeStruct((places, VARS, 1, LANES), F32),
        in_specs=[smem, vmem, hbm, hbm],
        out_specs=vmem,
        scratch_shapes=[
            pltpu.VMEM((81, 16, LANES), F32),
            pltpu.VMEM((2, ROWS, LANES), F32),
            pltpu.SMEM((places,), I32),
            dma((2,)),
        ],
        name="blend",
    )(meta, work, ext, own)

    return pl.pallas_call(
        functools.partial(reply_kernel, bins, doms, blocks),
        out_shape=jax.ShapeDtypeStruct((VARS, points.shape[1]), F32),
        in_specs=[smem, smem, vmem],
        out_specs=vmem,
        scratch_shapes=[
            pltpu.VMEM((places, VARS, 1, LANES), F32),
            pltpu.VMEM((count, VARS, 1, LANES), F32),
            pltpu.VMEM((count, VARS, 1, LANES), F32),
            pltpu.VMEM((blocks, VARS, 1, LANES), F32),
            pltpu.VMEM((blocks, VARS, 1, LANES), F32),
            dma, *routes, *pairs,
        ],
        compiler_params=pltpu.CompilerParams(collective_id=1, has_side_effects=True),
        name="reply",
    )(block_bin, meta, result)


def solution(mesh):
    split = P(None, ("dom", "bin"))
    table = P(("dom", "bin"))
    return jax.shard_map(
        local,
        mesh=mesh,
        in_specs=(split, split, table, table, table, split, split),
        out_specs=split,
        check_vma=False,
    )
```

```python
import functools

import jax
import jax.numpy as jnp
import numpy as np
from jax import lax
from jax.experimental import pallas as pl
from jax.experimental.pallas import tpu as pltpu
from jax.sharding import PartitionSpec as P

VARS = 5
LANES = 128
STEPS = 6
CAP_DOM = 2
X_CHIPS, CORES = 4, 2

NEAR = 4
GIVE = 3
SPREAD = NEAR * CORES
SHARE = 4
LENT = GIVE * SPREAD
NODE_ROWS, FLOW_ROWS = 88, 136
ROWS = NODE_ROWS + FLOW_ROWS

clamp_edge = 1.25
relax_factor = 0.5
sharpness = 16.0

MESH = pl.DeviceIdType.MESH
F32 = jnp.float32
I32 = jnp.int32


def monomial_map(fields, rows):
    one = np.array([[0.0, 1.0, 0.0], [-0.5, 0.0, 0.5], [0.5, -1.0, 0.5]])
    cell = np.kron(np.kron(one, one), one)
    full = np.kron(np.eye(fields), cell)
    return np.pad(full, ((0, rows - full.shape[0]), (0, 0)))


def exact_dot(left, right):
    high = right.astype(jnp.bfloat16)
    rest = right - high.astype(F32)
    mid = rest.astype(jnp.bfloat16)
    low = (rest - mid.astype(F32)).astype(jnp.bfloat16)
    out = jnp.dot(left, low, preferred_element_type=F32)
    out = out + jnp.dot(left, mid, preferred_element_type=F32)
    return out + jnp.dot(left, high, preferred_element_type=F32)


class Place:
    def __init__(self, bins, doms):
        self.bins, self.doms = bins, doms
        self.dom, self.bin = lax.axis_index("dom"), lax.axis_index("bin")
        self.core = lax.rem(self.dom, CORES)
        self.x = lax.rem(self.dom // CORES, X_CHIPS)
        self.z = self.dom // (CORES * X_CHIPS)

    def chip(self, near, core):
        step = 1 if near % 2 == 0 else -1
        layers = self.doms // (CORES * X_CHIPS)
        z, x = self.z, self.x
        if near < 2:
            z = lax.rem(z + step + layers, layers)
        else:
            x = lax.rem(x + step + X_CHIPS, X_CHIPS)
        return ((z * X_CHIPS + x) * CORES + core, self.bin)

    def sibling(self):
        return (self.dom + 1 - 2 * self.core, self.bin)

    def enter(self):
        barrier = pltpu.get_barrier_semaphore()

        def greet(device):
            pl.semaphore_signal(barrier, inc=1, device_id=device, device_id_type=MESH)

        def greet_bin(off, carry):
            greet((self.dom, lax.rem(self.bin + off, self.bins)))
            return carry

        def greet_dom(off, carry):
            greet((lax.rem(self.dom + off, self.doms), self.bin))
            return carry

        lax.fori_loop(1, self.bins, greet_bin, 0)
        lax.fori_loop(1, self.doms, greet_dom, 0)
        return lambda: pl.semaphore_wait(barrier, self.bins - 1 + self.doms - 1)


def holder(owner, slot, doms):
    layers = doms // (CORES * X_CHIPS)
    core = owner & (CORES - 1)
    x = (owner >> 1) & (X_CHIPS - 1)
    z = owner >> 3
    unit = (slot * 43) >> 7
    near, side = unit >> 1, unit & 1
    z = z + jnp.where(near == 0, 1, 0) - jnp.where(near == 1, 1, 0)
    x = x + jnp.where(near == 2, 1, 0) - jnp.where(near == 3, 1, 0)
    away = (lax.rem(z + layers, layers) * X_CHIPS + (x & (X_CHIPS - 1))) * CORES + side
    number = (near * CORES + core) * GIVE + slot - unit * GIVE
    lent = slot < LENT
    other = owner + 1 - 2 * core
    return (
        jnp.where(lent, away, jnp.where(slot < LENT + SHARE, other, owner)),
        jnp.where(lent, number, slot),
    )


def exchange(count, copy_to):
    def start(off, carry):
        copy_to(off).start()
        return carry

    def finish(off, carry):
        copy_to(off).wait()
        return carry

    lax.fori_loop(1, count, start, 0)
    return lambda: lax.fori_loop(1, count, finish, 0)


def ranks(labels):
    count = len(labels)
    out = []
    for i in range(count):
        rank = jnp.int32(0)
        for j in range(i):
            rank = rank + (labels[j] == labels[i]).astype(I32)
        out.append(rank)
    return out


def request_kernel(
    bins, doms, blocks, cells,
    bin_ref, dom_ref, slot_ref, pts_ref, cand_ref, node_map_ref, flow_map_ref, nodes_ref, flow_ref,
    tiles, meta_ref, all_ref,
    raw, msg, got, pack, node_raw, flow_raw, coef,
    load_sem, keep_sem, bin_send, bin_recv, dom_send, dom_recv, cell_send, cell_recv,
):
    me = Place(bins, doms)
    per = blocks // bins
    parts = load_sem.shape[1]
    width = cells // parts
    step = 256

    def load(i):
        span = pl.ds(i * width, width)
        return (
            pltpu.make_async_copy(nodes_ref.at[:, span], node_raw.at[:, span], load_sem.at[0, i]),
            pltpu.make_async_copy(flow_ref.at[:, span], flow_raw.at[:, span], load_sem.at[1, i]),
        )

    for i in range(parts):
        for copy in load(i):
            copy.start()
    entered = me.enter()
    sub = lax.broadcasted_iota(I32, (8, LANES), 0)
    lane = lax.broadcasted_iota(I32, (8, LANES), 1)

    for b in range(blocks):
        span = pl.ds(b * LANES, LANES)
        corner = jnp.min(cand_ref[:, span], axis=0, keepdims=True)
        raw[b, 0:3, :] = pts_ref[:, span]
        raw[b, 3:4, :] = corner.astype(F32)
        owner, slot = dom_ref[b], slot_ref[b]
        device, number = holder(owner, slot, doms)
        home = jnp.where(slot < LENT + SHARE, slot + cells // LANES, slot)
        for k, word in enumerate((owner, device, home, number)):
            raw[b, 4 + k : 5 + k, :] = jnp.full((1, LANES), word, I32).astype(F32)
    bin_of = [bin_ref[b] for b in range(blocks)]
    place = [x * per + r for x, r in zip(bin_of, ranks(bin_of))]
    for p in range(blocks):
        source = jnp.int32(0)
        for b in range(blocks):
            source = source + jnp.where(place[b] == p, b, 0)
        msg[p] = raw[source]

    def convert(i, carry):
        span = pl.ds(pl.multiple_of(i * step, step), step)
        node = exact_dot(node_map_ref[...], node_raw[:, span])
        flow = exact_dot(flow_map_ref[...], flow_raw[:, span])
        for k in range(step // LANES):
            part = slice(k * LANES, (k + 1) * LANES)
            coef[i * (step // LANES) + k, 0:NODE_ROWS, :] = node[:, part]
            coef[i * (step // LANES) + k, NODE_ROWS:ROWS, :] = flow[:, part]
        return carry

    for i in range(parts):
        for copy in load(i):
            copy.wait()
        lax.fori_loop(i * width // step, (i + 1) * width // step, convert, 0)
    first_kept, held = LENT + SHARE, cells // LANES
    keep = [
        pltpu.make_async_copy(coef, all_ref.at[pl.ds(held, held)], keep_sem.at[0]),
        pltpu.make_async_copy(
            coef.at[first_kept:], all_ref.at[pl.ds(first_kept, held - first_kept)], keep_sem.at[1]
        ),
    ]
    entered()

    def to_bin(off):
        other = lax.rem(me.bin + off, bins)
        return pltpu.make_async_remote_copy(
            src_ref=msg.at[pl.ds(other * per, per)],
            dst_ref=got.at[pl.ds(me.bin * per, per)],
            send_sem=bin_send.at[off],
            recv_sem=bin_recv.at[off],
            device_id=(me.dom, other),
            device_id_type=MESH,
        )

    finish_bin = exchange(bins, to_bin)

    spread = []
    for unit in range(SPREAD):
        near, core = unit // CORES, unit % CORES
        spread.append(
            pltpu.make_async_remote_copy(
                src_ref=coef.at[pl.ds(GIVE * unit, GIVE)],
                dst_ref=all_ref.at[pl.ds(GIVE * (near * CORES + me.core), GIVE)],
                send_sem=cell_send.at[unit],
                recv_sem=cell_recv.at[near * CORES + me.core],
                device_id=me.chip(near, core),
                device_id_type=MESH,
            )
        )
    spread.append(
        pltpu.make_async_remote_copy(
            src_ref=coef.at[pl.ds(LENT, SHARE)],
            dst_ref=all_ref.at[pl.ds(LENT, SHARE)],
            send_sem=cell_send.at[SPREAD],
            recv_sem=cell_recv.at[SPREAD],
            device_id=me.sibling(),
            device_id_type=MESH,
        )
    )
    for copy in spread:
        copy.start()
    for copy in keep:
        copy.start()

    for i in range(per):
        got[me.bin * per + i] = msg[me.bin * per + i]
    finish_bin()

    def line(b, r):
        return jnp.broadcast_to(got[b, r : r + 1, :], (8, LANES))

    owners = [line(b, 4) for b in range(blocks)]
    holders = [line(b, 5) for b in range(blocks)]
    goes, named, tile_of = [], [], []
    where_row = jnp.zeros((8, LANES), I32)
    for b in range(blocks):
        load = jnp.zeros((8, LANES), F32)
        for j in range(blocks):
            load = load + jnp.where(owners[j] == holders[b], 1.0, 0.0)
        for j in range(b):
            load = load + jnp.where(holders[j] == holders[b], 1.0, 0.0)
        moves = (load < CAP_DOM) & (holders[b] != owners[b])
        goes.append(jnp.where(moves, holders[b], owners[b]))
        number = jnp.where(moves | (holders[b] == owners[b]), line(b, 7), line(b, 6))
        rank = jnp.zeros((8, LANES), F32)
        for j in range(b):
            rank = rank + jnp.where(goes[j] == goes[b], 1.0, 0.0)
        named.append(jnp.where(jnp.where(sub < 4, 0.0, 1.0) == rank, goes[b], -1.0))
        tile = got[b]
        tile = jnp.where(sub == 3, tile + number * LANES, tile)
        tile_of.append(jnp.where(sub < 4, tile, pltpu.roll(tile, 4, 0)))
        where_row = jnp.where(lane == b, (goes[b] * CAP_DOM + rank).astype(I32), where_row)
    empty = jnp.where(sub % 4 == 3, -1.0, 0.0)

    def fill(a, carry):
        target = a.astype(F32)
        acc = empty
        for b in range(blocks):
            acc = jnp.where(named[b] == target, tile_of[b], acc)
        pack[a] = acc
        return carry

    lax.fori_loop(0, doms, fill, 0)

    def to_dom(off):
        other = lax.rem(me.dom + off, doms)
        return pltpu.make_async_remote_copy(
            src_ref=pack.at[other],
            dst_ref=tiles.at[pl.ds(pl.multiple_of(8 * me.dom, 8), 8)],
            send_sem=dom_send.at[off],
            recv_sem=dom_recv.at[off],
            device_id=(other, me.bin),
            device_id_type=MESH,
        )

    finish_dom = exchange(doms, to_dom)
    tiles[pl.ds(pl.multiple_of(8 * me.dom, 8), 8), :] = pack[me.dom]
    finish_dom()

    count = doms * CAP_DOM
    square = (count, LANES)
    first = lax.broadcasted_iota(I32, square, 0)
    second = lax.broadcasted_iota(I32, square, 1)
    block = jnp.floor(tiles[pl.ds(3, count, stride=4), :] * (1.0 / LANES))
    there = jnp.where(block >= 0.0, 1.0, 0.0)
    rank = jnp.sum(jnp.where(first < second, there, 0.0), axis=0, keepdims=True)
    rank = jnp.broadcast_to(rank, square).T
    chosen = (rank == second.astype(F32)) & (block >= 0.0)
    order = jnp.sum(jnp.where(chosen, first.astype(F32), 0.0), axis=0, keepdims=True)
    number = jnp.sum(jnp.where(chosen, block, 0.0), axis=0, keepdims=True)
    total = jnp.sum(there, axis=0, keepdims=True)
    table = where_row
    for i, words in ((0, order), (1, number), (2, total)):
        table = jnp.where(sub == i, jnp.broadcast_to(words, sub.shape).astype(I32), table)
    meta_ref[...] = table

    def arrived(unit, ref):
        pltpu.make_async_remote_copy(
            src_ref=ref, dst_ref=ref, send_sem=cell_recv.at[unit], recv_sem=cell_recv.at[unit],
            device_id=me.sibling(), device_id_type=MESH,
        ).wait_recv()

    for copy in spread:
        copy.wait_send()
    for unit in range(SPREAD):
        arrived(unit, all_ref.at[pl.ds(GIVE * unit, GIVE)])
    arrived(SPREAD, all_ref.at[pl.ds(LENT, SHARE)])
    for copy in keep:
        copy.wait()


def horner(t, c0, c1, c2):
    return (c2 * t + c1) * t + c0


def horner_slope(t, c0, c1, c2):
    top = c2 * t
    mid = top + c1
    return mid * t + c0, mid + top


def cross(a, b):
    return (
        a[1] * b[2] - a[2] * b[1],
        a[2] * b[0] - a[0] * b[2],
        a[0] * b[1] - a[1] * b[0],
    )


def dot3(a, b):
    return a[0] * b[0] + a[1] * b[1] + a[2] * b[2]


def blend_kernel(
    meta_ref, tiles_ref, all_ref,
    out_ref,
    held_even, held_odd, part_even, part_odd, cells_even, cells_odd, buf, sem,
):
    found = meta_ref[2, 0]
    sides = buf.shape[0]
    row = lax.broadcasted_iota(I32, (8, LANES), 0)
    box = 8 * (row // 4) + row % 4

    def fetch(n):
        n = jnp.minimum(n, found - 1)
        side = lax.rem(n, sides)
        return pltpu.make_async_copy(all_ref.at[meta_ref[1, n]], buf.at[side], sem.at[side])

    def locate(n, cells):
        n = jnp.clip(n, 0, found - 1)
        cell = tiles_ref[pl.ds(4 * meta_ref[0, n] + 3, 1), :].astype(I32) & (LANES - 1)
        corner = jnp.broadcast_to(cell, (8, LANES)) + box
        cells[0:8] = corner
        cells[8:16] = corner + 32

    def gather(n, held, cells):
        side = lax.rem(jnp.minimum(n, found - 1), sides)
        rows = [*range(81), *range(NODE_ROWS, NODE_ROWS + 135)]
        left = [(r, slice(8 * h, 8 * h + 8)) for h in range(2) for r in rows]
        where = [cells[0:8], cells[8:16]]

        def some(count):
            for _ in range(min(count, len(left))):
                r, part = left.pop(0)
                line = jnp.broadcast_to(buf[side, r : r + 1, :], (8, LANES))
                held[r, part] = jnp.take_along_axis(
                    line, where[part.start // 8], axis=1, mode="promise_in_bounds"
                )

        return some

    def solve(n, held, part, some):
        place = meta_ref[0, n]
        points = [
            jnp.broadcast_to(tiles_ref[pl.ds(4 * place + c, 1), :], (16, LANES)) for c in range(3)
        ]

        def coeff(c, i, j, k):
            return held[27 * c + 9 * i + 3 * j + k]

        r = None
        for step in range(STEPS):
            value, d1, d2, d3 = [], [], [], []
            for c in range(3):
                if r is None:
                    value.append(coeff(c, 0, 0, 0))
                    d1.append(coeff(c, 1, 0, 0))
                    d2.append(coeff(c, 0, 1, 0))
                    d3.append(coeff(c, 0, 0, 1))
                    continue
                x0, x2, x3 = [], [], []
                for i in range(3):
                    y0, y3 = [], []
                    for j in range(3):
                        v, d = horner_slope(r[2], *[coeff(c, i, j, k) for k in range(3)])
                        y0.append(v)
                        y3.append(d)
                        some(3)
                    v, d = horner_slope(r[1], *y0)
                    x0.append(v)
                    x2.append(d)
                    x3.append(horner(r[1], *y3))
                v, d = horner_slope(r[0], *x0)
                value.append(v)
                d1.append(d)
                d2.append(horner(r[0], *x2))
                d3.append(horner(r[0], *x3))
            misfit = [value[c] - points[c] for c in range(3)]
            normal = cross(d2, d3)
            side = cross(d1, misfit)
            scale = relax_factor / dot3(d1, normal)
            change = (dot3(misfit, normal), dot3(d3, side), -dot3(d2, side))
            r = [
                jnp.clip((0.0 if r is None else r[c]) - scale * change[c], -clamp_edge, clamp_edge)
                for c in range(3)
            ]
        excess = [jnp.maximum(jnp.abs(x) - 1.0, 0.0) for x in r]
        trust = 1.0 / (1.0 + sharpness * dot3(excess, excess))
        some(2 * ROWS)
        part[VARS] = trust[0:8] + trust[8:16]
        for v in range(VARS):
            x0 = []
            for i in range(3):
                y0 = []
                for j in range(3):
                    y0.append(
                        horner(
                            r[2],
                            *[held[NODE_ROWS + 27 * v + 9 * i + 3 * j + k] for k in range(3)],
                        )
                    )
                x0.append(horner(r[1], *y0))
            field = horner(r[0], *x0) * trust
            part[v] = field[0:8] + field[8:16]

    def settle(n, part):
        place = meta_ref[0, jnp.maximum(n, 0)]
        total = 1.0 / jnp.sum(part[VARS], axis=0, keepdims=True)
        for v in range(VARS):
            out_ref[place, v] = jnp.sum(part[v], axis=0, keepdims=True) * total

    @pl.when(found > 0)
    def _():
        for n in range(sides - 1):
            @pl.when(n < found)
            def _():
                fetch(n).start()
        fetch(0).wait()
        locate(0, cells_even)
        locate(1, cells_odd)
        gather(0, held_even, cells_even)(2 * ROWS)

    def half(n, held, part, cells, held_next, part_last, cells_next):
        @pl.when(n + sides - 1 < found)
        def _():
            fetch(n + sides - 1).start()

        @pl.when(n + 1 < found)
        def _():
            fetch(n + 1).wait()

        some = gather(n + 1, held_next, cells_next)
        locate(n + 2, cells)
        some(30)
        settle(n - 1, part_last)
        solve(n, held, part, some)

    def pair(p, carry):
        n = 2 * p
        half(n, held_even, part_even, cells_even, held_odd, part_odd, cells_odd)

        @pl.when(n + 1 < found)
        def _():
            half(n + 1, held_odd, part_odd, cells_odd, held_even, part_even, cells_even)

        return carry

    lax.fori_loop(0, (found + 1) // 2, pair, 0)

    @pl.when((found > 0) & (lax.rem(found, 2) == 1))
    def _():
        settle(found - 1, part_even)

    @pl.when((found > 0) & (lax.rem(found, 2) == 0))
    def _():
        settle(found - 1, part_odd)


def reply_kernel(
    bins, doms, blocks,
    bin_ref, meta_ref, res_ref,
    out_ref,
    back, picked, final, bin_send, bin_recv, dom_send, dom_recv,
):
    me = Place(bins, doms)
    per = blocks // bins
    me.enter()()

    def to_dom(off):
        other = lax.rem(me.dom + off, doms)
        return pltpu.make_async_remote_copy(
            src_ref=res_ref.at[pl.ds(CAP_DOM * other, CAP_DOM)],
            dst_ref=back.at[pl.ds(CAP_DOM * me.dom, CAP_DOM)],
            send_sem=dom_send.at[off],
            recv_sem=dom_recv.at[off],
            device_id=(other, me.bin),
            device_id_type=MESH,
        )

    finish = exchange(doms, to_dom)
    for k in range(CAP_DOM):
        back[CAP_DOM * me.dom + k] = res_ref[CAP_DOM * me.dom + k]
    finish()
    for b in range(blocks):
        picked[b] = back[meta_ref[3, b]]

    def to_bin(off):
        other = lax.rem(me.bin + off, bins)
        return pltpu.make_async_remote_copy(
            src_ref=picked.at[pl.ds(other * per, per)],
            dst_ref=final.at[pl.ds(me.bin * per, per)],
            send_sem=bin_send.at[off],
            recv_sem=bin_recv.at[off],
            device_id=(me.dom, other),
            device_id_type=MESH,
        )

    finish = exchange(bins, to_bin)
    for i in range(per):
        final[me.bin * per + i] = picked[me.bin * per + i]
    finish()
    bin_of = [bin_ref[b] for b in range(blocks)]
    place = [x * per + r for x, r in zip(bin_of, ranks(bin_of))]
    for b in range(blocks):
        out_ref[:, pl.ds(b * LANES, LANES)] = final[place[b]].reshape(VARS, LANES)


def local(points, candidates, block_dom, block_bin, block_slot, donor_nodes, donor_flow):
    bins, doms = lax.axis_size("bin"), lax.axis_size("dom")
    blocks = block_dom.shape[0]
    cells = donor_nodes.shape[1]
    held_blocks = cells // LANES
    count = doms * CAP_DOM
    vmem = pl.BlockSpec(memory_space=pltpu.VMEM)
    smem = pl.BlockSpec(memory_space=pltpu.SMEM)
    hbm = pl.BlockSpec(memory_space=pl.ANY)
    dma = pltpu.SemaphoreType.DMA
    routes = [dma((bins,)), dma((bins,)), dma((doms,)), dma((doms,))]
    node_map = jnp.asarray(monomial_map(3, NODE_ROWS), jnp.bfloat16)
    flow_map = jnp.asarray(monomial_map(VARS, FLOW_ROWS), jnp.bfloat16)

    tiles, meta, coefs = pl.pallas_call(
        functools.partial(request_kernel, bins, doms, blocks, cells),
        out_shape=(
            jax.ShapeDtypeStruct((doms * 8, LANES), F32),
            jax.ShapeDtypeStruct((8, LANES), I32),
            jax.ShapeDtypeStruct((2 * held_blocks, ROWS, LANES), F32),
        ),
        in_specs=[smem, smem, smem, vmem, vmem, vmem, vmem, hbm, hbm],
        out_specs=(vmem, vmem, hbm),
        scratch_shapes=[
            pltpu.VMEM((blocks, 8, LANES), F32),
            pltpu.VMEM((blocks, 8, LANES), F32),
            pltpu.VMEM((blocks, 8, LANES), F32),
            pltpu.VMEM((doms, 8, LANES), F32),
            pltpu.VMEM((81, cells), F32),
            pltpu.VMEM((135, cells), F32),
            pltpu.VMEM((held_blocks, ROWS, LANES), F32),
            dma((2, 4)), dma((2,)), *routes, dma((SPREAD + 1,)), dma((SPREAD + 1,)),
        ],
        compiler_params=pltpu.CompilerParams(collective_id=0, has_side_effects=True),
        name="request",
    )(
        block_bin, block_dom, block_slot, points, candidates, node_map, flow_map,
        donor_nodes, donor_flow,
    )

    result = pl.pallas_call(
        blend_kernel,
        out_shape=jax.ShapeDtypeStruct((count, VARS, 1, LANES), F32),
        in_specs=[smem, vmem, hbm],
        out_specs=vmem,
        scratch_shapes=[
            pltpu.VMEM((ROWS, 16, LANES), F32),
            pltpu.VMEM((ROWS, 16, LANES), F32),
            pltpu.VMEM((VARS + 1, 8, LANES), F32),
            pltpu.VMEM((VARS + 1, 8, LANES), F32),
            pltpu.VMEM((16, LANES), I32),
            pltpu.VMEM((16, LANES), I32),
            pltpu.VMEM((4, ROWS, LANES), F32),
            dma((4,)),
        ],
        name="blend",
    )(meta, tiles, coefs)

    return pl.pallas_call(
        functools.partial(reply_kernel, bins, doms, blocks),
        out_shape=jax.ShapeDtypeStruct((VARS, points.shape[1]), F32),
        in_specs=[smem, smem, vmem],
        out_specs=vmem,
        scratch_shapes=[
            pltpu.VMEM((count, VARS, 1, LANES), F32),
            pltpu.VMEM((blocks, VARS, 1, LANES), F32),
            pltpu.VMEM((blocks, VARS, 1, LANES), F32),
            *routes,
        ],
        compiler_params=pltpu.CompilerParams(collective_id=1, has_side_effects=True),
        name="reply",
    )(block_bin, meta, result)


def solution(mesh):
    split = P(None, ("dom", "bin"))
    table = P(("dom", "bin"))
    return jax.shard_map(
        local,
        mesh=mesh,
        in_specs=(split, split, table, table, table, split, split),
        out_specs=split,
        check_vma=False,
    )
```

```python
import functools

import jax
import jax.numpy as jnp
import numpy as np
from jax import lax
from jax.experimental import pallas as pl
from jax.experimental.pallas import tpu as pltpu
from jax.sharding import PartitionSpec as P

VARS = 5
LANES = 128
STEPS = 6
CAP_DOM = 2
X_CHIPS, CORES = 4, 2

NEAR = 4
GIVE = (3, 3, 3, 3)
SPREAD = NEAR * CORES
SHARE = 4
START = tuple(CORES * sum(GIVE[:near]) for near in range(NEAR + 1))
LENT = START[NEAR]
NODE_ROWS, FLOW_ROWS = 88, 136
ROWS = 216
EARLY = 1

clamp_edge = 1.25
relax_factor = 0.5
sharpness = 16.0

MESH = pl.DeviceIdType.MESH
F32 = jnp.float32
I32 = jnp.int32


def monomial_map(fields, rows):
    one = np.array([[0.0, 1.0, 0.0], [-0.5, 0.0, 0.5], [0.5, -1.0, 0.5]])
    cell = np.kron(np.kron(one, one), one)
    full = np.kron(np.eye(fields), cell)
    return np.pad(full, ((0, rows - full.shape[0]), (0, 0)))


def exact_dot(left, right):
    high = right.astype(jnp.bfloat16)
    rest = right - high.astype(F32)
    mid = rest.astype(jnp.bfloat16)
    low = (rest - mid.astype(F32)).astype(jnp.bfloat16)
    out = jnp.dot(left, low, preferred_element_type=F32)
    out = out + jnp.dot(left, mid, preferred_element_type=F32)
    return out + jnp.dot(left, high, preferred_element_type=F32)


class Place:
    def __init__(self, bins, doms):
        self.bins, self.doms = bins, doms
        self.dom, self.bin = lax.axis_index("dom"), lax.axis_index("bin")
        self.core = lax.rem(self.dom, CORES)
        self.x = lax.rem(self.dom // CORES, X_CHIPS)
        self.z = self.dom // (CORES * X_CHIPS)

    def chip(self, near, core):
        step = 1 if near % 2 == 0 else -1
        layers = self.doms // (CORES * X_CHIPS)
        z, x = self.z, self.x
        if near < 2:
            z = lax.rem(z + step + layers, layers)
        else:
            x = lax.rem(x + step + X_CHIPS, X_CHIPS)
        return ((z * X_CHIPS + x) * CORES + core, self.bin)

    def sibling(self):
        return (self.dom + 1 - 2 * self.core, self.bin)

    def enter(self):
        barrier = pltpu.get_barrier_semaphore()

        def greet(device):
            pl.semaphore_signal(barrier, inc=1, device_id=device, device_id_type=MESH)

        def greet_bin(off, carry):
            greet((self.dom, lax.rem(self.bin + off, self.bins)))
            return carry

        def greet_dom(off, carry):
            greet((lax.rem(self.dom + off, self.doms), self.bin))
            return carry

        lax.fori_loop(1, self.bins, greet_bin, 0)
        lax.fori_loop(1, self.doms, greet_dom, 0)
        return lambda: pl.semaphore_wait(barrier, self.bins - 1 + self.doms - 1)


def holder(owner, slot, doms):
    layers = doms // (CORES * X_CHIPS)
    core = owner & (CORES - 1)
    x = (owner >> 1) & (X_CHIPS - 1)
    z = owner >> 3
    near, start, give = 0, START[0], GIVE[0]
    for n in range(1, NEAR):
        past = slot >= START[n]
        near = jnp.where(past, n, near)
        start = jnp.where(past, START[n], start)
        give = jnp.where(past, GIVE[n], give)
    side = jnp.where(slot - start >= give, 1, 0)
    z = z + jnp.where(near == 0, 1, 0) - jnp.where(near == 1, 1, 0)
    x = x + jnp.where(near == 2, 1, 0) - jnp.where(near == 3, 1, 0)
    away = (lax.rem(z + layers, layers) * X_CHIPS + (x & (X_CHIPS - 1))) * CORES + side
    number = slot + (core - side) * give
    lent = slot < LENT
    other = owner + 1 - 2 * core
    return (
        jnp.where(lent, away, jnp.where(slot < LENT + SHARE, other, owner)),
        jnp.where(lent, number, slot),
    )


def exchange(count, copy_to):
    def start(off, carry):
        copy_to(off).start()
        return carry

    def finish(off, carry):
        copy_to(off).wait()
        return carry

    lax.fori_loop(1, count, start, 0)
    return lambda: lax.fori_loop(1, count, finish, 0)


def ranks(labels):
    count = len(labels)
    out = []
    for i in range(count):
        rank = jnp.int32(0)
        for j in range(i):
            rank = rank + (labels[j] == labels[i]).astype(I32)
        out.append(rank)
    return out


def request_kernel(
    bins, doms, blocks, cells,
    bin_ref, dom_ref, slot_ref, pts_ref, cand_ref, node_map_ref, flow_map_ref, nodes_ref, flow_ref,
    tiles, meta_ref, all_ref,
    raw, msg, got, pack, node_raw, flow_raw, coef,
    load_sem, keep_sem, bin_send, bin_recv, dom_send, dom_recv, cell_send, cell_recv,
):
    me = Place(bins, doms)
    per = blocks // bins
    parts = load_sem.shape[1]
    width = cells // parts
    step = 256

    def load(i):
        span = pl.ds(i * width, width)
        return (
            pltpu.make_async_copy(nodes_ref.at[:, span], node_raw.at[:, span], load_sem.at[0, i]),
            pltpu.make_async_copy(flow_ref.at[:, span], flow_raw.at[:, span], load_sem.at[1, i]),
        )

    for i in range(parts):
        for copy in load(i):
            copy.start()
    entered = me.enter()
    sub = lax.broadcasted_iota(I32, (8, LANES), 0)
    lane = lax.broadcasted_iota(I32, (8, LANES), 1)

    for b in range(blocks):
        span = pl.ds(b * LANES, LANES)
        corner = jnp.min(cand_ref[:, span], axis=0, keepdims=True)
        raw[b, 0:3, :] = pts_ref[:, span]
        raw[b, 3:4, :] = corner.astype(F32)
        owner, slot = dom_ref[b], slot_ref[b]
        device, number = holder(owner, slot, doms)
        home = jnp.where(slot < LENT + SHARE, slot + cells // LANES, slot)
        for k, word in enumerate((owner, device, home, number)):
            raw[b, 4 + k : 5 + k, :] = jnp.full((1, LANES), word, I32).astype(F32)
    bin_of = [bin_ref[b] for b in range(blocks)]
    place = [x * per + r for x, r in zip(bin_of, ranks(bin_of))]
    for p in range(blocks):
        source = jnp.int32(0)
        for b in range(blocks):
            source = source + jnp.where(place[b] == p, b, 0)
        msg[p] = raw[source]

    def convert(i, carry):
        span = pl.ds(pl.multiple_of(i * step, step), step)
        node = exact_dot(node_map_ref[...], node_raw[:, span])
        flow = exact_dot(flow_map_ref[...], flow_raw[:, span])
        for k in range(step // LANES):
            part = slice(k * LANES, (k + 1) * LANES)
            block = i * (step // LANES) + k
            coef[block, 0:FLOW_ROWS, :] = flow[:, part]
            coef[block, FLOW_ROWS - 1 : FLOW_ROWS, :] = node[80:81, part]
            coef[block, FLOW_ROWS:ROWS, :] = node[0:80, part]
        return carry

    def prepare(i):
        for copy in load(i):
            copy.wait()
        lax.fori_loop(i * width // step, (i + 1) * width // step, convert, 0)

    for i in range(parts - 1):
        prepare(i)
    first_kept, held = LENT + SHARE, cells // LANES
    keep = [
        pltpu.make_async_copy(coef, all_ref.at[pl.ds(held, held)], keep_sem.at[0]),
        pltpu.make_async_copy(
            coef.at[first_kept:], all_ref.at[pl.ds(first_kept, held - first_kept)], keep_sem.at[1]
        ),
    ]
    entered()

    def to_bin(off):
        other = lax.rem(me.bin + off, bins)
        return pltpu.make_async_remote_copy(
            src_ref=msg.at[pl.ds(other * per, per)],
            dst_ref=got.at[pl.ds(me.bin * per, per)],
            send_sem=bin_send.at[off],
            recv_sem=bin_recv.at[off],
            device_id=(me.dom, other),
            device_id_type=MESH,
        )

    finish_bin = exchange(bins, to_bin)

    def lend(unit, first, last, sem):
        near, core = unit // CORES, unit % CORES
        return pltpu.make_async_remote_copy(
            src_ref=coef.at[pl.ds(START[near] + core * GIVE[near] + first, last - first)],
            dst_ref=all_ref.at[pl.ds(START[near] + me.core * GIVE[near] + first, last - first)],
            send_sem=cell_send.at[sem + unit],
            recv_sem=cell_recv.at[sem + near * CORES + me.core],
            device_id=me.chip(near, core),
            device_id_type=MESH,
        )

    early = [lend(unit, 0, EARLY, 0) for unit in range(SPREAD)] if EARLY else []
    late = [lend(unit, EARLY, GIVE[unit // CORES], SPREAD) for unit in range(SPREAD)]
    other_core = pltpu.make_async_remote_copy(
        src_ref=coef.at[pl.ds(LENT, SHARE)],
        dst_ref=all_ref.at[pl.ds(LENT, SHARE)],
        send_sem=cell_send.at[2 * SPREAD],
        recv_sem=cell_recv.at[2 * SPREAD],
        device_id=me.sibling(),
        device_id_type=MESH,
    )
    for copy in early:
        copy.start()
    prepare(parts - 1)
    other_core.start()
    for copy in keep:
        copy.start()

    for i in range(per):
        got[me.bin * per + i] = msg[me.bin * per + i]
    finish_bin()

    def line(b, r):
        return jnp.broadcast_to(got[b, r : r + 1, :], (8, LANES))

    owners = [line(b, 4) for b in range(blocks)]
    holders = [line(b, 5) for b in range(blocks)]
    goes, named, tile_of = [], [], []
    where_row = jnp.zeros((8, LANES), I32)
    for b in range(blocks):
        load = jnp.zeros((8, LANES), F32)
        for j in range(blocks):
            load = load + jnp.where(owners[j] == holders[b], 1.0, 0.0)
        for j in range(b):
            load = load + jnp.where(holders[j] == holders[b], 1.0, 0.0)
        moves = (load < CAP_DOM) & (holders[b] != owners[b])
        goes.append(jnp.where(moves, holders[b], owners[b]))
        number = jnp.where(moves | (holders[b] == owners[b]), line(b, 7), line(b, 6))
        rank = jnp.zeros((8, LANES), F32)
        for j in range(b):
            rank = rank + jnp.where(goes[j] == goes[b], 1.0, 0.0)
        named.append(jnp.where(jnp.where(sub < 4, 0.0, 1.0) == rank, goes[b], -1.0))
        tile = got[b]
        tile = jnp.where(sub == 3, tile + number * LANES, tile)
        tile_of.append(jnp.where(sub < 4, tile, pltpu.roll(tile, 4, 0)))
        where_row = jnp.where(lane == b, (goes[b] * CAP_DOM + rank).astype(I32), where_row)
    empty = jnp.where(sub % 4 == 3, -1.0, 0.0)

    def fill(a, carry):
        target = a.astype(F32)
        acc = empty
        for b in range(blocks):
            acc = jnp.where(named[b] == target, tile_of[b], acc)
        pack[a] = acc
        return carry

    lax.fori_loop(0, doms, fill, 0)

    def to_dom(off):
        other = lax.rem(me.dom + off, doms)
        return pltpu.make_async_remote_copy(
            src_ref=pack.at[other],
            dst_ref=tiles.at[pl.ds(pl.multiple_of(8 * me.dom, 8), 8)],
            send_sem=dom_send.at[off],
            recv_sem=dom_recv.at[off],
            device_id=(other, me.bin),
            device_id_type=MESH,
        )

    finish_dom = exchange(doms, to_dom)
    for copy in late:
        copy.start()
    tiles[pl.ds(pl.multiple_of(8 * me.dom, 8), 8), :] = pack[me.dom]
    finish_dom()

    count = doms * CAP_DOM
    square = (count, LANES)
    first = lax.broadcasted_iota(I32, square, 0)
    second = lax.broadcasted_iota(I32, square, 1)
    block = jnp.floor(tiles[pl.ds(3, count, stride=4), :] * (1.0 / LANES))
    there = jnp.where(block >= 0.0, 1.0, 0.0)
    rank = jnp.sum(jnp.where(first < second, there, 0.0), axis=0, keepdims=True)
    rank = jnp.broadcast_to(rank, square).T
    chosen = (rank == second.astype(F32)) & (block >= 0.0)
    order = jnp.sum(jnp.where(chosen, first.astype(F32), 0.0), axis=0, keepdims=True)
    number = jnp.sum(jnp.where(chosen, block, 0.0), axis=0, keepdims=True)
    total = jnp.sum(there, axis=0, keepdims=True)
    table = where_row
    for i, words in ((0, order), (1, number), (2, total)):
        table = jnp.where(sub == i, jnp.broadcast_to(words, sub.shape).astype(I32), table)
    meta_ref[...] = table

    def arrived(unit, ref):
        pltpu.make_async_remote_copy(
            src_ref=ref, dst_ref=ref, send_sem=cell_recv.at[unit], recv_sem=cell_recv.at[unit],
            device_id=me.sibling(), device_id_type=MESH,
        ).wait_recv()

    for copy in [*early, *late, other_core]:
        copy.wait_send()
    for unit in range(SPREAD):
        near, core = unit // CORES, unit % CORES
        start = START[near] + core * GIVE[near]
        if EARLY:
            arrived(unit, all_ref.at[pl.ds(start, EARLY)])
        arrived(SPREAD + unit, all_ref.at[pl.ds(start + EARLY, GIVE[near] - EARLY)])
    arrived(2 * SPREAD, all_ref.at[pl.ds(LENT, SHARE)])
    for copy in keep:
        copy.wait()


def horner(t, c0, c1, c2):
    return (c2 * t + c1) * t + c0


def horner_slope(t, c0, c1, c2):
    top = c2 * t
    mid = top + c1
    return mid * t + c0, mid + top


def cross(a, b):
    return (
        a[1] * b[2] - a[2] * b[1],
        a[2] * b[0] - a[0] * b[2],
        a[0] * b[1] - a[1] * b[0],
    )


def dot3(a, b):
    return a[0] * b[0] + a[1] * b[1] + a[2] * b[2]


def blend_kernel(
    meta_ref, tiles_ref, all_ref,
    out_ref,
    held_even, held_odd, part_even, part_odd, cells_even, cells_odd, buf, sem,
):
    found = meta_ref[2, 0]
    sides = buf.shape[0]
    row = lax.broadcasted_iota(I32, (8, LANES), 0)
    box = 8 * (row // 4) + row % 4

    def fetch(n):
        n = jnp.minimum(n, found - 1)
        side = lax.rem(n, sides)
        return pltpu.make_async_copy(all_ref.at[meta_ref[1, n]], buf.at[side, pl.ds(0, ROWS)], sem.at[side])

    def locate(n, cells):
        n = jnp.clip(n, 0, found - 1)
        cell = tiles_ref[pl.ds(4 * meta_ref[0, n] + 3, 1), :].astype(I32) & (LANES - 1)
        corner = jnp.broadcast_to(cell, (8, LANES)) + box
        cells[0:8] = corner
        cells[8:16] = corner + 32

    def gather(n, held, cells):
        side = lax.rem(jnp.minimum(n, found - 1), sides)
        rows = [*range(FLOW_ROWS - 1, ROWS), *range(FLOW_ROWS - 1)]
        left = [(r, slice(8 * h, 8 * h + 8)) for h in range(2) for r in rows]
        where = [cells[0:8], cells[8:16]]

        def some(count):
            for _ in range(min(count, len(left))):
                r, part = left.pop(0)
                line = jnp.broadcast_to(buf[side, r : r + 1, :], (8, LANES))
                held[r, part] = jnp.take_along_axis(
                    line, where[part.start // 8], axis=1, mode="promise_in_bounds"
                )

        return some

    def solve(n, held, part, some):
        place = meta_ref[0, n]
        points = [
            jnp.broadcast_to(tiles_ref[pl.ds(4 * place + c, 1), :], (16, LANES)) for c in range(3)
        ]

        def coeff(c, i, j, k):
            at = 27 * c + 9 * i + 3 * j + k
            return held[FLOW_ROWS + at if at < 80 else FLOW_ROWS - 1]

        r = None
        for step in range(STEPS):
            value, d1, d2, d3 = [], [], [], []
            for c in range(3):
                if r is None:
                    value.append(coeff(c, 0, 0, 0))
                    d1.append(coeff(c, 1, 0, 0))
                    d2.append(coeff(c, 0, 1, 0))
                    d3.append(coeff(c, 0, 0, 1))
                    continue
                x0, x2, x3 = [], [], []
                for i in range(3):
                    y0, y3 = [], []
                    for j in range(3):
                        v, d = horner_slope(r[2], *[coeff(c, i, j, k) for k in range(3)])
                        y0.append(v)
                        y3.append(d)
                        some(3)
                    v, d = horner_slope(r[1], *y0)
                    x0.append(v)
                    x2.append(d)
                    x3.append(horner(r[1], *y3))
                v, d = horner_slope(r[0], *x0)
                value.append(v)
                d1.append(d)
                d2.append(horner(r[0], *x2))
                d3.append(horner(r[0], *x3))
            misfit = [value[c] - points[c] for c in range(3)]
            normal = cross(d2, d3)
            side = cross(d1, misfit)
            scale = relax_factor / dot3(d1, normal)
            change = (dot3(misfit, normal), dot3(d3, side), -dot3(d2, side))
            r = [
                jnp.clip((0.0 if r is None else r[c]) - scale * change[c], -clamp_edge, clamp_edge)
                for c in range(3)
            ]
        excess = [jnp.maximum(jnp.abs(x) - 1.0, 0.0) for x in r]
        trust = 1.0 / (1.0 + sharpness * dot3(excess, excess))
        some(2 * ROWS)
        part[VARS] = trust[0:8] + trust[8:16]
        for v in range(VARS):
            x0 = []
            for i in range(3):
                y0 = []
                for j in range(3):
                    y0.append(
                        horner(
                            r[2],
                            *[held[27 * v + 9 * i + 3 * j + k] for k in range(3)],
                        )
                    )
                x0.append(horner(r[1], *y0))
            field = horner(r[0], *x0) * trust
            part[v] = field[0:8] + field[8:16]

    def settle(n, part):
        place = meta_ref[0, jnp.maximum(n, 0)]
        total = 1.0 / jnp.sum(part[VARS], axis=0, keepdims=True)
        for v in range(VARS):
            out_ref[place, v] = jnp.sum(part[v], axis=0, keepdims=True) * total

    @pl.when(found > 0)
    def _():
        for n in range(sides - 1):
            @pl.when(n < found)
            def _():
                fetch(n).start()
        fetch(0).wait()
        locate(0, cells_even)
        locate(1, cells_odd)
        gather(0, held_even, cells_even)(2 * ROWS)

    def half(n, held, part, cells, held_next, part_last, cells_next):
        @pl.when(n + sides - 1 < found)
        def _():
            fetch(n + sides - 1).start()

        @pl.when(n + 1 < found)
        def _():
            fetch(n + 1).wait()

        some = gather(n + 1, held_next, cells_next)
        locate(n + 2, cells)
        some(30)
        solve(n, held, part, some)
        settle(n - 1, part_last)

    def pair(p, carry):
        n = 2 * p
        half(n, held_even, part_even, cells_even, held_odd, part_odd, cells_odd)

        @pl.when(n + 1 < found)
        def _():
            half(n + 1, held_odd, part_odd, cells_odd, held_even, part_even, cells_even)

        return carry

    lax.fori_loop(0, (found + 1) // 2, pair, 0)

    @pl.when((found > 0) & (lax.rem(found, 2) == 1))
    def _():
        settle(found - 1, part_even)

    @pl.when((found > 0) & (lax.rem(found, 2) == 0))
    def _():
        settle(found - 1, part_odd)


def reply_kernel(
    bins, doms, blocks,
    bin_ref, meta_ref, res_ref,
    out_ref,
    back, picked, final, bin_send, bin_recv, dom_send, dom_recv,
):
    me = Place(bins, doms)
    per = blocks // bins
    entered = me.enter()
    bin_of = [bin_ref[b] for b in range(blocks)]
    place = [x * per + r for x, r in zip(bin_of, ranks(bin_of))]
    entered()

    def to_dom(off):
        other = lax.rem(me.dom + off, doms)
        return pltpu.make_async_remote_copy(
            src_ref=res_ref.at[pl.ds(CAP_DOM * other, CAP_DOM)],
            dst_ref=back.at[pl.ds(CAP_DOM * me.dom, CAP_DOM)],
            send_sem=dom_send.at[off],
            recv_sem=dom_recv.at[off],
            device_id=(other, me.bin),
            device_id_type=MESH,
        )

    finish = exchange(doms, to_dom)
    for k in range(CAP_DOM):
        back[CAP_DOM * me.dom + k] = res_ref[CAP_DOM * me.dom + k]
    finish()
    for b in range(blocks):
        picked[b] = back[meta_ref[3, b]]

    def to_bin(off):
        other = lax.rem(me.bin + off, bins)
        return pltpu.make_async_remote_copy(
            src_ref=picked.at[pl.ds(other * per, per)],
            dst_ref=final.at[pl.ds(me.bin * per, per)],
            send_sem=bin_send.at[off],
            recv_sem=bin_recv.at[off],
            device_id=(me.dom, other),
            device_id_type=MESH,
        )

    finish = exchange(bins, to_bin)
    for i in range(per):
        final[me.bin * per + i] = picked[me.bin * per + i]
    finish()
    for b in range(blocks):
        out_ref[:, pl.ds(b * LANES, LANES)] = final[place[b]].reshape(VARS, LANES)


def local(points, candidates, block_dom, block_bin, block_slot, donor_nodes, donor_flow):
    bins, doms = lax.axis_size("bin"), lax.axis_size("dom")
    blocks = block_dom.shape[0]
    cells = donor_nodes.shape[1]
    held_blocks = cells // LANES
    count = doms * CAP_DOM
    vmem = pl.BlockSpec(memory_space=pltpu.VMEM)
    smem = pl.BlockSpec(memory_space=pltpu.SMEM)
    hbm = pl.BlockSpec(memory_space=pl.ANY)
    dma = pltpu.SemaphoreType.DMA
    routes = [dma((bins,)), dma((bins,)), dma((doms,)), dma((doms,))]
    node_map = jnp.asarray(monomial_map(3, NODE_ROWS), jnp.bfloat16)
    flow_map = jnp.asarray(monomial_map(VARS, FLOW_ROWS), jnp.bfloat16)

    tiles, meta, coefs = pl.pallas_call(
        functools.partial(request_kernel, bins, doms, blocks, cells),
        out_shape=(
            jax.ShapeDtypeStruct((doms * 8, LANES), F32),
            jax.ShapeDtypeStruct((8, LANES), I32),
            jax.ShapeDtypeStruct((2 * held_blocks, ROWS, LANES), F32),
        ),
        in_specs=[smem, smem, smem, vmem, vmem, vmem, vmem, hbm, hbm],
        out_specs=(vmem, vmem, hbm),
        scratch_shapes=[
            pltpu.VMEM((blocks, 8, LANES), F32),
            pltpu.VMEM((blocks, 8, LANES), F32),
            pltpu.VMEM((blocks, 8, LANES), F32),
            pltpu.VMEM((doms, 8, LANES), F32),
            pltpu.VMEM((81, cells), F32),
            pltpu.VMEM((135, cells), F32),
            pltpu.VMEM((held_blocks, ROWS, LANES), F32),
            dma((2, 4)), dma((2,)), *routes, dma((2 * SPREAD + 1,)), dma((2 * SPREAD + 1,)),
        ],
        compiler_params=pltpu.CompilerParams(collective_id=0, has_side_effects=True),
        name="request",
    )(
        block_bin, block_dom, block_slot, points, candidates, node_map, flow_map,
        donor_nodes, donor_flow,
    )

    result = pl.pallas_call(
        blend_kernel,
        out_shape=jax.ShapeDtypeStruct((count, VARS, 1, LANES), F32),
        in_specs=[smem, vmem, hbm],
        out_specs=vmem,
        scratch_shapes=[
            pltpu.VMEM((224, 16, LANES), F32),
            pltpu.VMEM((224, 16, LANES), F32),
            pltpu.VMEM((VARS + 1, 8, LANES), F32),
            pltpu.VMEM((VARS + 1, 8, LANES), F32),
            pltpu.VMEM((16, LANES), I32),
            pltpu.VMEM((16, LANES), I32),
            pltpu.VMEM((4, 224, LANES), F32),
            dma((4,)),
        ],
        compiler_params=pltpu.CompilerParams(

        ),
        name="blend",
    )(meta, tiles, coefs)

    return pl.pallas_call(
        functools.partial(reply_kernel, bins, doms, blocks),
        out_shape=jax.ShapeDtypeStruct((VARS, points.shape[1]), F32),
        in_specs=[smem, smem, vmem],
        out_specs=vmem,
        scratch_shapes=[
            pltpu.VMEM((count, VARS, 1, LANES), F32),
            pltpu.VMEM((blocks, VARS, 1, LANES), F32),
            pltpu.VMEM((blocks, VARS, 1, LANES), F32),
            *routes,
        ],
        compiler_params=pltpu.CompilerParams(collective_id=1, has_side_effects=True),
        name="reply",
    )(block_bin, meta, result)


def solution(mesh):
    split = P(None, ("dom", "bin"))
    table = P(("dom", "bin"))
    return jax.shard_map(
        local,
        mesh=mesh,
        in_specs=(split, split, table, table, table, split, split),
        out_specs=split,
        check_vma=False,
    )
```

```python
import functools

import jax
import jax.numpy as jnp
import numpy as np
from jax import lax
from jax.experimental import pallas as pl
from jax.experimental.pallas import tpu as pltpu
from jax.sharding import PartitionSpec as P

VARS = 5
LANES = 128
STEPS = 6
CAP_DOM = 2
X_CHIPS, CORES = 4, 2

NEAR = 4
SPREAD = NEAR * CORES
EARLY, LATE = 2, 1
SHARE = 4
LENT = (EARLY + LATE) * SPREAD
NODE_ROWS, FLOW_ROWS = 88, 136
ROWS = 216

clamp_edge = 1.25
relax_factor = 0.5
sharpness = 16.0

MESH = pl.DeviceIdType.MESH
F32 = jnp.float32
I32 = jnp.int32


def monomial_map(fields, rows):
    one = np.array([[0.0, 1.0, 0.0], [-0.5, 0.0, 0.5], [0.5, -1.0, 0.5]])
    cell = np.kron(np.kron(one, one), one)
    full = np.kron(np.eye(fields), cell)
    return np.pad(full, ((0, rows - full.shape[0]), (0, 0)))


def exact_dot(left, right):
    high = right.astype(jnp.bfloat16)
    rest = right - high.astype(F32)
    mid = rest.astype(jnp.bfloat16)
    low = (rest - mid.astype(F32)).astype(jnp.bfloat16)
    out = jnp.dot(left, low, preferred_element_type=F32)
    out = out + jnp.dot(left, mid, preferred_element_type=F32)
    return out + jnp.dot(left, high, preferred_element_type=F32)


class Place:
    def __init__(self, bins, doms):
        self.bins, self.doms = bins, doms
        self.dom, self.bin = lax.axis_index("dom"), lax.axis_index("bin")
        self.core = lax.rem(self.dom, CORES)
        self.x = lax.rem(self.dom // CORES, X_CHIPS)
        self.z = self.dom // (CORES * X_CHIPS)

    def chip(self, near, core):
        step = 1 if near % 2 == 0 else -1
        layers = self.doms // (CORES * X_CHIPS)
        z, x = self.z, self.x
        if near < 2:
            z = lax.rem(z + step + layers, layers)
        else:
            x = lax.rem(x + step + X_CHIPS, X_CHIPS)
        return ((z * X_CHIPS + x) * CORES + core, self.bin)

    def sibling(self):
        return (self.dom + 1 - 2 * self.core, self.bin)

    def enter_near(self):
        barrier = pltpu.get_barrier_semaphore()
        devices = [(self.dom, lax.rem(self.bin + off, self.bins)) for off in range(1, self.bins)]
        devices += [self.chip(near, core) for near in range(NEAR) for core in range(CORES)]
        devices += [self.sibling()]
        for device in devices:
            pl.semaphore_signal(barrier, inc=1, device_id=device, device_id_type=MESH)
        return lambda: pl.semaphore_wait(barrier, len(devices))

    def rounds(self, sem):
        layers = self.doms // (CORES * X_CHIPS)
        along = [[self.chip(0, self.core), self.chip(1, self.core)]] * (layers // 2 - 1)
        along += [[self.chip(2, self.core), self.chip(3, self.core)]] * (X_CHIPS // 2)
        along += [[self.sibling()]]

        def signal(k):
            for device in along[k]:
                pl.semaphore_signal(sem.at[k], inc=1, device_id=device, device_id_type=MESH)

        return len(along), signal, lambda k: pl.semaphore_wait(sem.at[k], len(along[k]))

    def enter(self):
        barrier = pltpu.get_barrier_semaphore()

        def greet(device):
            pl.semaphore_signal(barrier, inc=1, device_id=device, device_id_type=MESH)

        def greet_bin(off, carry):
            greet((self.dom, lax.rem(self.bin + off, self.bins)))
            return carry

        def greet_dom(off, carry):
            greet((lax.rem(self.dom + off, self.doms), self.bin))
            return carry

        lax.fori_loop(1, self.bins, greet_bin, 0)
        lax.fori_loop(1, self.doms, greet_dom, 0)
        return lambda: pl.semaphore_wait(barrier, self.bins - 1 + self.doms - 1)


def holder(owner, slot, doms):
    layers = doms // (CORES * X_CHIPS)
    core = owner & (CORES - 1)
    x = (owner >> 1) & (X_CHIPS - 1)
    z = owner >> 3
    early = slot < EARLY * SPREAD
    unit = jnp.where(early, slot >> 1, slot - EARLY * SPREAD)
    near, side = unit >> 1, unit & 1
    z = z + jnp.where(near == 0, 1, 0) - jnp.where(near == 1, 1, 0)
    x = x + jnp.where(near == 2, 1, 0) - jnp.where(near == 3, 1, 0)
    away = (lax.rem(z + layers, layers) * X_CHIPS + (x & (X_CHIPS - 1))) * CORES + side
    number = slot + (core - side) * jnp.where(early, EARLY, LATE)
    lent = slot < LENT
    other = owner + 1 - 2 * core
    return (
        jnp.where(lent, away, jnp.where(slot < LENT + SHARE, other, owner)),
        jnp.where(lent, number, slot),
    )


def exchange(count, copy_to):
    def start(off, carry):
        copy_to(off).start()
        return carry

    def finish(off, carry):
        copy_to(off).wait()
        return carry

    lax.fori_loop(1, count, start, 0)
    return lambda: lax.fori_loop(1, count, finish, 0)


def ranks(labels):
    count = len(labels)
    out = []
    for i in range(count):
        rank = jnp.int32(0)
        for j in range(i):
            rank = rank + (labels[j] == labels[i]).astype(I32)
        out.append(rank)
    return out


def request_kernel(
    bins, doms, blocks, cells,
    bin_ref, dom_ref, slot_ref, pts_ref, cand_ref, node_map_ref, flow_map_ref, nodes_ref, flow_ref,
    tiles, meta_ref, all_ref,
    raw, msg, got, pack, node_raw, flow_raw, coef,
    load_sem, keep_sem, bin_send, bin_recv, dom_send, dom_recv, cell_send, cell_recv, round_sem,
):
    me = Place(bins, doms)
    per = blocks // bins
    parts = load_sem.shape[1]
    width = cells // parts
    step = 256

    def load(i):
        span = pl.ds(i * width, width)
        return (
            pltpu.make_async_copy(nodes_ref.at[:, span], node_raw.at[:, span], load_sem.at[0, i]),
            pltpu.make_async_copy(flow_ref.at[:, span], flow_raw.at[:, span], load_sem.at[1, i]),
        )

    for i in range(parts):
        for copy in load(i):
            copy.start()
    entered = me.enter_near()
    last, signal, wait = me.rounds(round_sem)
    sub = lax.broadcasted_iota(I32, (8, LANES), 0)
    lane = lax.broadcasted_iota(I32, (8, LANES), 1)

    for b in range(blocks):
        span = pl.ds(b * LANES, LANES)
        corner = jnp.min(cand_ref[:, span], axis=0, keepdims=True)
        raw[b, 0:3, :] = pts_ref[:, span]
        raw[b, 3:4, :] = corner.astype(F32)
        owner, slot = dom_ref[b], slot_ref[b]
        device, number = holder(owner, slot, doms)
        home = jnp.where(slot < LENT + SHARE, slot + cells // LANES, slot)
        for k, word in enumerate((owner, device, home, number)):
            raw[b, 4 + k : 5 + k, :] = jnp.full((1, LANES), word, I32).astype(F32)
    bin_of = [bin_ref[b] for b in range(blocks)]
    place = [x * per + r for x, r in zip(bin_of, ranks(bin_of))]
    for p in range(blocks):
        source = jnp.int32(0)
        for b in range(blocks):
            source = source + jnp.where(place[b] == p, b, 0)
        msg[p] = raw[source]

    def convert(i, carry):
        span = pl.ds(pl.multiple_of(i * step, step), step)
        node = exact_dot(node_map_ref[...], node_raw[:, span])
        flow = exact_dot(flow_map_ref[...], flow_raw[:, span])
        for k in range(step // LANES):
            part = slice(k * LANES, (k + 1) * LANES)
            block = i * (step // LANES) + k
            coef[block, 0:FLOW_ROWS, :] = flow[:, part]
            coef[block, FLOW_ROWS - 1 : FLOW_ROWS, :] = node[80:81, part]
            coef[block, FLOW_ROWS:ROWS, :] = node[0:80, part]
        return carry

    def prepare(i):
        for copy in load(i):
            copy.wait()
        lax.fori_loop(i * width // step, (i + 1) * width // step, convert, 0)

    prepare(0)
    first_kept, held = LENT + SHARE, cells // LANES
    keep = [
        pltpu.make_async_copy(coef, all_ref.at[pl.ds(held, held)], keep_sem.at[0]),
        pltpu.make_async_copy(
            coef.at[first_kept:], all_ref.at[pl.ds(first_kept, held - first_kept)], keep_sem.at[1]
        ),
    ]
    entered()

    def to_bin(off):
        other = lax.rem(me.bin + off, bins)
        return pltpu.make_async_remote_copy(
            src_ref=msg.at[pl.ds(other * per, per)],
            dst_ref=got.at[pl.ds(me.bin * per, per)],
            send_sem=bin_send.at[off],
            recv_sem=bin_recv.at[off],
            device_id=(me.dom, other),
            device_id_type=MESH,
        )

    finish_bin = exchange(bins, to_bin)

    def early_at(unit):
        return pl.ds(EARLY * unit, EARLY)

    def late_at(unit):
        return pl.ds(EARLY * SPREAD + LATE * unit, LATE)

    def lend(unit, at, sem):
        near, core = unit // CORES, unit % CORES
        return pltpu.make_async_remote_copy(
            src_ref=coef.at[at(unit)],
            dst_ref=all_ref.at[at(near * CORES + me.core)],
            send_sem=cell_send.at[sem + unit],
            recv_sem=cell_recv.at[sem + near * CORES + me.core],
            device_id=me.chip(near, core),
            device_id_type=MESH,
        )

    early = [lend(unit, early_at, 0) for unit in range(SPREAD)]
    late = [lend(unit, late_at, SPREAD) for unit in range(SPREAD)]
    other_core = pltpu.make_async_remote_copy(
        src_ref=coef.at[pl.ds(LENT, SHARE)],
        dst_ref=all_ref.at[pl.ds(LENT, SHARE)],
        send_sem=cell_send.at[2 * SPREAD],
        recv_sem=cell_recv.at[2 * SPREAD],
        device_id=me.sibling(),
        device_id_type=MESH,
    )
    for copy in early[: SPREAD // 2]:
        copy.start()
    for i in range(1, parts):
        signal(i - 1)
        prepare(i)
        if i == 1:
            for copy in early[SPREAD // 2 :]:
                copy.start()
        wait(i - 1)
    signal(parts - 1)
    other_core.start()
    for copy in keep:
        copy.start()

    for i in range(per):
        got[me.bin * per + i] = msg[me.bin * per + i]
    finish_bin()

    def line(b, r):
        return jnp.broadcast_to(got[b, r : r + 1, :], (8, LANES))

    owners = [line(b, 4) for b in range(blocks)]
    holders = [line(b, 5) for b in range(blocks)]
    goes, named, tile_of = [], [], []
    where_row = jnp.zeros((8, LANES), I32)
    for b in range(blocks):
        load = jnp.zeros((8, LANES), F32)
        for j in range(blocks):
            load = load + jnp.where(owners[j] == holders[b], 1.0, 0.0)
        for j in range(b):
            load = load + jnp.where(holders[j] == holders[b], 1.0, 0.0)
        moves = (load < CAP_DOM) & (holders[b] != owners[b])
        goes.append(jnp.where(moves, holders[b], owners[b]))
        number = jnp.where(moves | (holders[b] == owners[b]), line(b, 7), line(b, 6))
        rank = jnp.zeros((8, LANES), F32)
        for j in range(b):
            rank = rank + jnp.where(goes[j] == goes[b], 1.0, 0.0)
        named.append(jnp.where(jnp.where(sub < 4, 0.0, 1.0) == rank, goes[b], -1.0))
        tile = got[b]
        tile = jnp.where(sub == 3, tile + number * LANES, tile)
        tile_of.append(jnp.where(sub < 4, tile, pltpu.roll(tile, 4, 0)))
        where_row = jnp.where(lane == b, (goes[b] * CAP_DOM + rank).astype(I32), where_row)
    empty = jnp.where(sub % 4 == 3, -1.0, 0.0)

    wait(parts - 1)
    signal(parts)

    def fill(a, carry):
        target = a.astype(F32)
        acc = empty
        for b in range(blocks):
            acc = jnp.where(named[b] == target, tile_of[b], acc)
        pack[a] = acc
        return carry

    lax.fori_loop(0, doms, fill, 0)

    wait(parts)
    for k in range(parts + 1, last):
        signal(k)
        wait(k)

    def to_dom(off):
        other = lax.rem(me.dom + off, doms)
        return pltpu.make_async_remote_copy(
            src_ref=pack.at[other],
            dst_ref=tiles.at[pl.ds(pl.multiple_of(8 * me.dom, 8), 8)],
            send_sem=dom_send.at[off],
            recv_sem=dom_recv.at[off],
            device_id=(other, me.bin),
            device_id_type=MESH,
        )

    finish_dom = exchange(doms, to_dom)
    for copy in late:
        copy.start()
    tiles[pl.ds(pl.multiple_of(8 * me.dom, 8), 8), :] = pack[me.dom]
    finish_dom()

    count = doms * CAP_DOM
    square = (count, LANES)
    first = lax.broadcasted_iota(I32, square, 0)
    second = lax.broadcasted_iota(I32, square, 1)
    block = jnp.floor(tiles[pl.ds(3, count, stride=4), :] * (1.0 / LANES))
    there = jnp.where(block >= 0.0, 1.0, 0.0)
    rank = jnp.sum(jnp.where(first < second, there, 0.0), axis=0, keepdims=True)
    rank = jnp.broadcast_to(rank, square).T
    chosen = (rank == second.astype(F32)) & (block >= 0.0)
    order = jnp.sum(jnp.where(chosen, first.astype(F32), 0.0), axis=0, keepdims=True)
    number = jnp.sum(jnp.where(chosen, block, 0.0), axis=0, keepdims=True)
    total = jnp.sum(there, axis=0, keepdims=True)
    table = where_row
    for i, words in ((0, order), (1, number), (2, total)):
        table = jnp.where(sub == i, jnp.broadcast_to(words, sub.shape).astype(I32), table)
    meta_ref[...] = table

    def arrived(unit, ref):
        pltpu.make_async_remote_copy(
            src_ref=ref, dst_ref=ref, send_sem=cell_recv.at[unit], recv_sem=cell_recv.at[unit],
            device_id=me.sibling(), device_id_type=MESH,
        ).wait_recv()

    for copy in [*early, *late, other_core]:
        copy.wait_send()
    for unit in range(SPREAD):
        arrived(unit, all_ref.at[early_at(unit)])
        arrived(SPREAD + unit, all_ref.at[late_at(unit)])
    arrived(2 * SPREAD, all_ref.at[pl.ds(LENT, SHARE)])
    for copy in keep:
        copy.wait()


def horner(t, c0, c1, c2):
    return (c2 * t + c1) * t + c0


def horner_slope(t, c0, c1, c2):
    top = c2 * t
    mid = top + c1
    return mid * t + c0, mid + top


def cross(a, b):
    return (
        a[1] * b[2] - a[2] * b[1],
        a[2] * b[0] - a[0] * b[2],
        a[0] * b[1] - a[1] * b[0],
    )


def dot3(a, b):
    return a[0] * b[0] + a[1] * b[1] + a[2] * b[2]


def blend_kernel(
    meta_ref, tiles_ref, all_ref,
    out_ref,
    held_even, held_odd, part_even, part_odd, cells_even, cells_odd, buf, sem,
):
    found = meta_ref[2, 0]
    sides = buf.shape[0]
    row = lax.broadcasted_iota(I32, (8, LANES), 0)
    box = 8 * (row // 4) + row % 4

    def fetch(n):
        n = jnp.minimum(n, found - 1)
        side = lax.rem(n, sides)
        return pltpu.make_async_copy(all_ref.at[meta_ref[1, n]], buf.at[side, pl.ds(0, ROWS)], sem.at[side])

    def locate(n, cells):
        n = jnp.clip(n, 0, found - 1)
        cell = tiles_ref[pl.ds(4 * meta_ref[0, n] + 3, 1), :].astype(I32) & (LANES - 1)
        corner = jnp.broadcast_to(cell, (8, LANES)) + box
        cells[0:8] = corner
        cells[8:16] = corner + 32

    def gather(n, held, cells):
        side = lax.rem(jnp.minimum(n, found - 1), sides)
        rows = [*range(FLOW_ROWS - 1, ROWS), *range(FLOW_ROWS - 1)]
        left = [(r, slice(8 * h, 8 * h + 8)) for h in range(2) for r in rows]
        where = [cells[0:8], cells[8:16]]

        def some(count):
            for _ in range(min(count, len(left))):
                r, part = left.pop(0)
                line = jnp.broadcast_to(buf[side, r : r + 1, :], (8, LANES))
                held[r, part] = jnp.take_along_axis(
                    line, where[part.start // 8], axis=1, mode="promise_in_bounds"
                )

        return some

    def solve(n, held, part, some):
        place = meta_ref[0, n]
        points = [
            jnp.broadcast_to(tiles_ref[pl.ds(4 * place + c, 1), :], (16, LANES)) for c in range(3)
        ]

        def coeff(c, i, j, k):
            at = 27 * c + 9 * i + 3 * j + k
            return held[FLOW_ROWS + at if at < 80 else FLOW_ROWS - 1]

        r = None
        for step in range(STEPS):
            value, d1, d2, d3 = [], [], [], []
            for c in range(3):
                if r is None:
                    value.append(coeff(c, 0, 0, 0))
                    d1.append(coeff(c, 1, 0, 0))
                    d2.append(coeff(c, 0, 1, 0))
                    d3.append(coeff(c, 0, 0, 1))
                    continue
                x0, x2, x3 = [], [], []
                for i in range(3):
                    y0, y3 = [], []
                    for j in range(3):
                        v, d = horner_slope(r[2], *[coeff(c, i, j, k) for k in range(3)])
                        y0.append(v)
                        y3.append(d)
                        some(3)
                    v, d = horner_slope(r[1], *y0)
                    x0.append(v)
                    x2.append(d)
                    x3.append(horner(r[1], *y3))
                v, d = horner_slope(r[0], *x0)
                value.append(v)
                d1.append(d)
                d2.append(horner(r[0], *x2))
                d3.append(horner(r[0], *x3))
            misfit = [value[c] - points[c] for c in range(3)]
            normal = cross(d2, d3)
            side = cross(d1, misfit)
            scale = relax_factor / dot3(d1, normal)
            change = (dot3(misfit, normal), dot3(d3, side), -dot3(d2, side))
            r = [
                jnp.clip((0.0 if r is None else r[c]) - scale * change[c], -clamp_edge, clamp_edge)
                for c in range(3)
            ]
        excess = [jnp.maximum(jnp.abs(x) - 1.0, 0.0) for x in r]
        trust = 1.0 / (1.0 + sharpness * dot3(excess, excess))
        some(2 * ROWS)
        part[VARS] = trust[0:8] + trust[8:16]
        for v in range(VARS):
            x0 = []
            for i in range(3):
                y0 = []
                for j in range(3):
                    y0.append(
                        horner(
                            r[2],
                            *[held[27 * v + 9 * i + 3 * j + k] for k in range(3)],
                        )
                    )
                x0.append(horner(r[1], *y0))
            field = horner(r[0], *x0) * trust
            part[v] = field[0:8] + field[8:16]

    def settle(n, part):
        place = meta_ref[0, jnp.maximum(n, 0)]
        total = 1.0 / jnp.sum(part[VARS], axis=0, keepdims=True)
        for v in range(VARS):
            out_ref[place, v] = jnp.sum(part[v], axis=0, keepdims=True) * total

    @pl.when(found > 0)
    def _():
        for n in range(sides - 1):
            @pl.when(n < found)
            def _():
                fetch(n).start()
        fetch(0).wait()
        locate(0, cells_even)
        locate(1, cells_odd)
        gather(0, held_even, cells_even)(2 * ROWS)

    def half(n, held, part, cells, held_next, part_last, cells_next):
        @pl.when(n + sides - 1 < found)
        def _():
            fetch(n + sides - 1).start()

        @pl.when(n + 1 < found)
        def _():
            fetch(n + 1).wait()

        some = gather(n + 1, held_next, cells_next)
        locate(n + 2, cells)
        some(30)
        solve(n, held, part, some)
        settle(n - 1, part_last)

    def pair(p, carry):
        n = 2 * p
        half(n, held_even, part_even, cells_even, held_odd, part_odd, cells_odd)

        @pl.when(n + 1 < found)
        def _():
            half(n + 1, held_odd, part_odd, cells_odd, held_even, part_even, cells_even)

        return carry

    lax.fori_loop(0, (found + 1) // 2, pair, 0)

    @pl.when((found > 0) & (lax.rem(found, 2) == 1))
    def _():
        settle(found - 1, part_even)

    @pl.when((found > 0) & (lax.rem(found, 2) == 0))
    def _():
        settle(found - 1, part_odd)


def reply_kernel(
    bins, doms, blocks,
    bin_ref, meta_ref, res_ref,
    out_ref,
    back, picked, final, bin_send, bin_recv, dom_send, dom_recv,
):
    me = Place(bins, doms)
    per = blocks // bins
    entered = me.enter()
    bin_of = [bin_ref[b] for b in range(blocks)]
    place = [x * per + r for x, r in zip(bin_of, ranks(bin_of))]
    entered()

    def to_dom(off):
        other = lax.rem(me.dom + off, doms)
        return pltpu.make_async_remote_copy(
            src_ref=res_ref.at[pl.ds(CAP_DOM * other, CAP_DOM)],
            dst_ref=back.at[pl.ds(CAP_DOM * me.dom, CAP_DOM)],
            send_sem=dom_send.at[off],
            recv_sem=dom_recv.at[off],
            device_id=(other, me.bin),
            device_id_type=MESH,
        )

    finish = exchange(doms, to_dom)
    for k in range(CAP_DOM):
        back[CAP_DOM * me.dom + k] = res_ref[CAP_DOM * me.dom + k]
    finish()
    for b in range(blocks):
        picked[b] = back[meta_ref[3, b]]

    def to_bin(off):
        other = lax.rem(me.bin + off, bins)
        return pltpu.make_async_remote_copy(
            src_ref=picked.at[pl.ds(other * per, per)],
            dst_ref=final.at[pl.ds(me.bin * per, per)],
            send_sem=bin_send.at[off],
            recv_sem=bin_recv.at[off],
            device_id=(me.dom, other),
            device_id_type=MESH,
        )

    finish = exchange(bins, to_bin)
    for i in range(per):
        final[me.bin * per + i] = picked[me.bin * per + i]
    finish()
    for b in range(blocks):
        out_ref[:, pl.ds(b * LANES, LANES)] = final[place[b]].reshape(VARS, LANES)


def local(points, candidates, block_dom, block_bin, block_slot, donor_nodes, donor_flow):
    bins, doms = lax.axis_size("bin"), lax.axis_size("dom")
    blocks = block_dom.shape[0]
    cells = donor_nodes.shape[1]
    held_blocks = cells // LANES
    count = doms * CAP_DOM
    vmem = pl.BlockSpec(memory_space=pltpu.VMEM)
    smem = pl.BlockSpec(memory_space=pltpu.SMEM)
    hbm = pl.BlockSpec(memory_space=pl.ANY)
    dma = pltpu.SemaphoreType.DMA
    routes = [dma((bins,)), dma((bins,)), dma((doms,)), dma((doms,))]
    node_map = jnp.asarray(monomial_map(3, NODE_ROWS), jnp.bfloat16)
    flow_map = jnp.asarray(monomial_map(VARS, FLOW_ROWS), jnp.bfloat16)

    tiles, meta, coefs = pl.pallas_call(
        functools.partial(request_kernel, bins, doms, blocks, cells),
        out_shape=(
            jax.ShapeDtypeStruct((doms * 8, LANES), F32),
            jax.ShapeDtypeStruct((8, LANES), I32),
            jax.ShapeDtypeStruct((2 * held_blocks, ROWS, LANES), F32),
        ),
        in_specs=[smem, smem, smem, vmem, vmem, vmem, vmem, hbm, hbm],
        out_specs=(vmem, vmem, hbm),
        scratch_shapes=[
            pltpu.VMEM((blocks, 8, LANES), F32),
            pltpu.VMEM((blocks, 8, LANES), F32),
            pltpu.VMEM((blocks, 8, LANES), F32),
            pltpu.VMEM((doms, 8, LANES), F32),
            pltpu.VMEM((81, cells), F32),
            pltpu.VMEM((135, cells), F32),
            pltpu.VMEM((held_blocks, ROWS, LANES), F32),
            dma((2, 4)), dma((2,)), *routes, dma((2 * SPREAD + 1,)), dma((2 * SPREAD + 1,)),
            pltpu.SemaphoreType.REGULAR((8,)),
        ],
        compiler_params=pltpu.CompilerParams(collective_id=0, has_side_effects=True),
        name="request",
    )(
        block_bin, block_dom, block_slot, points, candidates, node_map, flow_map,
        donor_nodes, donor_flow,
    )

    result = pl.pallas_call(
        blend_kernel,
        out_shape=jax.ShapeDtypeStruct((count, VARS, 1, LANES), F32),
        in_specs=[smem, vmem, hbm],
        out_specs=vmem,
        scratch_shapes=[
            pltpu.VMEM((224, 16, LANES), F32),
            pltpu.VMEM((224, 16, LANES), F32),
            pltpu.VMEM((VARS + 1, 8, LANES), F32),
            pltpu.VMEM((VARS + 1, 8, LANES), F32),
            pltpu.VMEM((16, LANES), I32),
            pltpu.VMEM((16, LANES), I32),
            pltpu.VMEM((4, 224, LANES), F32),
            dma((4,)),
        ],
        compiler_params=pltpu.CompilerParams(

        ),
        name="blend",
    )(meta, tiles, coefs)

    return pl.pallas_call(
        functools.partial(reply_kernel, bins, doms, blocks),
        out_shape=jax.ShapeDtypeStruct((VARS, points.shape[1]), F32),
        in_specs=[smem, smem, vmem],
        out_specs=vmem,
        scratch_shapes=[
            pltpu.VMEM((count, VARS, 1, LANES), F32),
            pltpu.VMEM((blocks, VARS, 1, LANES), F32),
            pltpu.VMEM((blocks, VARS, 1, LANES), F32),
            *routes,
        ],
        compiler_params=pltpu.CompilerParams(collective_id=1, has_side_effects=True),
        name="reply",
    )(block_bin, meta, result)


def solution(mesh):
    split = P(None, ("dom", "bin"))
    table = P(("dom", "bin"))
    return jax.shard_map(
        local,
        mesh=mesh,
        in_specs=(split, split, table, table, table, split, split),
        out_specs=split,
        check_vma=False,
    )
```
